256 devices in a mesh: ctx: 64 (over y, z, core), vocab: 4 (over x).
Axes of the slice: x: 4, y: 4, z: 8, core: 2. Of those that a mesh axis runs over, the one named last changes fastest.
Arguments:
- hidden_states: bfloat16 [16384, 8192], P('ctx'), may hold values from -24 to 24
- master: float32 [1024, 8192], P(('vocab', 'ctx')), may hold values from -1 to 1
- moment: float32 [1024, 8192], P(('vocab', 'ctx')), may hold values from -6 to 6
- second: float32 [1024, 8192], P(('vocab', 'ctx')), may hold values from 0.05 to 5
- targets: int32 [16384], P('ctx'), may hold values from 0 to 2047, as said below
- loss_mask: int32 [16384], P('ctx'), may hold values from 0 to 1, as said below
- prior_lse: float32 [16384], P('ctx'), may hold values from 6 to 9
- prior_target: float32 [16384], P('ctx'), may hold values from -5 to 5
- span_order: int32 [128], replicated, may hold values from 0 to 127, as said below
Outputs:
- token_loss: float32 [16384], P('ctx')
- mean_loss: float32 [], replicated
- hidden_grad: bfloat16 [16384, 8192], P('ctx', 'vocab')
- new_master: float32 [1024, 8192], P(('vocab', 'ctx'))
- new_moment: float32 [1024, 8192], P(('vocab', 'ctx'))
- new_second: float32 [1024, 8192], P(('vocab', 'ctx'))
The draws below stay inside these ranges and needn't reach their ends.
Inputs may be any that keep to these rules, and one draw needn't show every extreme that they name: `targets`: ids of 1024 and more fall in this block, id minus 1024 naming its row; smaller ids lie in earlier blocks. `loss_mask`: 1 on a leading run of the slab's positions and 0 after it; at least 4096 ones. `span_order`: each span number once.
All inputs are finite; a program needn't handle non-finite values.
Results may differ from the reference program's by a relative error of at most 0.0085.
Values may be sent and summed in bfloat16 or wider, within the bound.
No kernel may reach another device: no remote copies, remote signals or barrier semaphores. Data moves between devices by JAX's collectives and lax.ppermute only.
A program may use at most 128 MiB of HBM per device.

```python
import math
import jax
import jax.numpy as jnp
from jax import lax

D = 8192
SPAN = 128
SPANS = 128
TOKENS = 16384
VBLOCK = 1024
N_VOCAB = 4


hit_rows = 16


per_row = 4


def head_table(key):
    return jnp.clip(jax.random.normal(key, (VBLOCK, D), jnp.float32), -6.0, 6.0) * D ** (-0.5)


def layout_order(key):
    return jax.random.permutation(jax.random.fold_in(key, 31), SPANS).astype(jnp.int32)


def target_ids(key):
    far_ids = jax.random.randint(jax.random.fold_in(key, 41), (TOKENS,), 0, VBLOCK, dtype=jnp.int32)
    far_ids = far_ids.at[TOKENS - 1].set(0)
    stride = VBLOCK // hit_rows
    jitter = jax.random.randint(jax.random.fold_in(key, 42), (hit_rows,), 0, stride, dtype=jnp.int32)
    jitter = jitter.at[0].set(0)
    block_rows = VBLOCK - 1 - jnp.arange(hit_rows, dtype=jnp.int32) * stride - jitter
    spots = jax.random.permutation(jax.random.fold_in(key, 43), TOKENS // 4)[:hit_rows * per_row].astype(jnp.int32)
    block_ids = jnp.repeat(block_rows, per_row) + VBLOCK
    return far_ids.at[spots].set(block_ids.astype(jnp.int32))


def draw_targets(key, part):
    return target_ids(key)


def draw_span_order(key, part):
    return layout_order(key)


def draw_master(key, part):
    return head_table(jax.random.fold_in(key, 11))


def draw_hidden_states(key, part):
    order = layout_order(key)
    row_pos = (order[:, None] * SPAN + jnp.arange(SPAN, dtype=jnp.int32)[None, :]).reshape(-1)
    row_targets = target_ids(key)[row_pos]
    cluster = jnp.clip(jax.random.normal(jax.random.fold_in(key, 51), (2 * VBLOCK, D), jnp.float32), -6.0, 6.0)
    shared = cluster[row_targets]
    base = jnp.clip(jax.random.normal(jax.random.fold_in(key, 1), (TOKENS, D), jnp.float32), -6.0, 6.0)
    base = jnp.clip(base + shared, -24.0, 24.0)
    return base.astype(jnp.bfloat16)


def draw_loss_mask(key, part):
    valid = jax.random.randint(key, (), TOKENS // 4, TOKENS + 1)
    return (jnp.arange(TOKENS, dtype=jnp.int32) < valid).astype(jnp.int32)


def shard_levels(stream_key, shape, shards, low, high):
    def one(axis_at, blocks):
        heights = jax.random.uniform(jax.random.fold_in(jax.random.fold_in(stream_key, 6), axis_at), (blocks,), jnp.float32, low / len(shards), high / len(shards))
        return jnp.repeat(jnp.exp(heights), shape[axis_at] // blocks).reshape((-1,) + (1,) * (len(shape) - axis_at - 1))

    gain = one(*shards[0])
    for cut in shards[1:]:
        gain = gain * one(*cut)
    return gain


def scatter_about(key, dims, spread, limit, shards=(), kind=jnp.bfloat16):
    entries = spread * jax.random.normal(key, dims, jnp.float32)
    if shards:
        entries = entries * shard_levels(key, dims, shards, -0.22, 0.18)
    return jnp.clip(entries, -limit, limit).astype(kind)


def setup_inputs(seed: int = 0) -> dict:
    splits = jax.random.split(jax.random.key(seed), 10)
    hidden_states = draw_hidden_states(jax.random.fold_in(splits[9], 71), 0)
    master = draw_master(jax.random.fold_in(splits[9], 71), 0)
    moment = scatter_about(splits[2], (VBLOCK, D), 1.0, 6.0, ((0, 256),), jnp.float32)
    second = jnp.clip(jnp.exp(math.log(5.0) - 4.6051702 * jax.random.uniform(splits[3], (VBLOCK, D), jnp.float32) ** shard_levels(splits[3], (VBLOCK, D), ((0, 256),), -0.2, 0.2)), 0.05, 5.0)
    targets = draw_targets(jax.random.fold_in(splits[9], 71), 0)
    loss_mask = draw_loss_mask(jax.random.fold_in(splits[9], 71), 0)
    prior_lse = jnp.clip(6.0 + 3.0 * jax.random.uniform(splits[6], (TOKENS,), jnp.float32) ** shard_levels(splits[6], (TOKENS,), ((0, 64),), -0.2, 0.2), 6.0, 9.0)
    prior_target = scatter_about(splits[7], (TOKENS,), 1.0, 5.0, ((0, 64),), jnp.float32)
    span_order = draw_span_order(jax.random.fold_in(splits[9], 71), 0)
    return {"hidden_states": hidden_states, "master": master, "moment": moment, "second": second, "targets": targets, "loss_mask": loss_mask, "prior_lse": prior_lse, "prior_target": prior_target, "span_order": span_order}


loss_scale = 1048576.0
clip_norm = 0.004
beta_one = 0.9
beta_two = 0.95
learn_rate = 0.001
weight_decay = 0.1
adam_eps = 1e-08

def reference(hidden_states, master, moment, second, targets, loss_mask, prior_lse, prior_target, span_order):
    row_pos = (span_order[:, None] * SPAN + jnp.arange(SPAN, dtype=jnp.int32)[None, :]).reshape(-1).astype(jnp.int32)
    tgt_rows = targets[row_pos]
    mask_rows = loss_mask[row_pos].astype(jnp.float32)
    prior_rows = prior_lse[row_pos]
    outside = prior_target[row_pos]
    head_rows = master.astype(jnp.bfloat16)
    logits = jnp.dot(hidden_states, head_rows.T, preferred_element_type=jnp.float32)
    columns = jnp.arange(VBLOCK, dtype=jnp.int32)
    onehot = (columns[None, :] == (tgt_rows - VBLOCK)[:, None]).astype(jnp.float32)
    inside = lax.optimization_barrier(jnp.sum(logits * onehot, axis=1))
    target_logit = jnp.where(tgt_rows >= VBLOCK, inside, outside)
    top_value = jnp.maximum(prior_rows, lax.optimization_barrier(jnp.max(logits, axis=1)))
    log_total = top_value + jnp.log(jnp.exp(prior_rows - top_value) + lax.optimization_barrier(jnp.sum(jnp.exp(logits - top_value[:, None]), axis=1)))
    token_count = jnp.sum(loss_mask.astype(jnp.float32))
    loss_rows = mask_rows * (log_total - target_logit)
    token_loss = jnp.zeros((TOKENS,), jnp.float32).at[row_pos].set(loss_rows)
    mean_loss = jnp.sum(loss_rows) / token_count
    grad_scale = loss_scale / token_count
    dlogits = (mask_rows[:, None] * (jnp.exp(logits - log_total[:, None]) - onehot) * grad_scale).astype(jnp.bfloat16)
    row_grad = jnp.dot(dlogits.T, hidden_states, preferred_element_type=jnp.float32)
    quarter = VBLOCK // N_VOCAB
    hidden_sum = jnp.zeros((TOKENS, D), jnp.float32)
    for part_index in range(N_VOCAB):
        lower = part_index * quarter
        partial_value = jnp.dot(dlogits[:, lower:lower + quarter], head_rows[lower:lower + quarter], preferred_element_type=jnp.float32).astype(jnp.bfloat16)
        partial_value = lax.optimization_barrier(partial_value)
        hidden_sum = hidden_sum + partial_value.astype(jnp.float32)
    hidden_grad = hidden_sum.astype(jnp.bfloat16)
    square_sum = jnp.sum(row_grad * row_grad)
    norm_value = jnp.sqrt(square_sum) / loss_scale
    clip_factor = jnp.minimum(1.0, clip_norm / (norm_value + 1e-06))
    clipped = row_grad * clip_factor
    new_moment = beta_one * moment + (1.0 - beta_one) * clipped
    new_second = beta_two * second + (1.0 - beta_two) * clipped * clipped
    new_master = master - learn_rate * (new_moment / (jnp.sqrt(new_second) + adam_eps) + weight_decay * master)
    return (token_loss, mean_loss, hidden_grad, new_master, new_moment, new_second)
```

```python
import jax
import jax.numpy as jnp
from jax import lax
from jax.sharding import Mesh, PartitionSpec as P

loss_scale = 1048576.0
clip_norm = 0.004
beta_one = 0.9
beta_two = 0.95
learn_rate = 0.001
weight_decay = 0.1
adam_eps = 1e-08

NY, NZ, NC = 4, 8, 2
CTX = ("y", "z", "core")
ALL = ("y", "z", "core", "vocab")
SWAP = [(0, 1), (1, 0)]
f32 = jnp.float32
bf16 = jnp.bfloat16


def exchange(x, axes):
    return lax.all_to_all(x, axes, 0, 0, tiled=True)


def spread(x, axes, count):
    return exchange(jnp.broadcast_to(x[None], (count,) + x.shape), axes)


def body(
    hidden_states, master, moment, second, targets, loss_mask, prior_lse, prior_target, span_order
):
    tok_rows, feat = hidden_states.shape
    shard_rows = master.shape[0]
    vocab_count = lax.axis_size("vocab")
    ctx_count = NY * NZ * NC
    core = lax.axis_index("core")
    vocab_place = lax.axis_index("vocab")
    ctx_place = (lax.axis_index("y") * NZ + lax.axis_index("z")) * NC + core
    span = tok_rows // 2
    half = feat // 2
    group_rows = shard_rows * ctx_count
    block_total = group_rows * vocab_count
    y_rows = group_rows // NY
    chip_rows = y_rows // NZ

    cut = master.astype(bf16).reshape(shard_rows, NC, half).transpose(1, 0, 2)
    cut = jnp.broadcast_to(cut[None], (NZ,) + cut.shape).reshape(NZ * NC, shard_rows, half)
    block = exchange(cut, ("z", "core")).reshape(y_rows, half)
    head = spread(block, "y", NY).reshape(group_rows, half)

    own_half = lax.dynamic_slice_in_dim(hidden_states, core * half, half, 1)
    far_half = lax.dynamic_slice_in_dim(hidden_states, (1 - core) * half, half, 1)
    mate_half = lax.ppermute(far_half, "core", SWAP)
    tokens = jnp.concatenate([own_half, mate_half], 0)

    small = jnp.concatenate(
        [
            targets.astype(f32).reshape(2, span),
            loss_mask.astype(f32).reshape(2, span),
            prior_lse.reshape(2, span),
            prior_target.reshape(2, span),
        ],
        0,
    )
    small = spread(small, CTX, ctx_count).reshape(ctx_count, 4, 2, span)
    token_count = jnp.sum(small[:, 1])
    pieces = []
    for offset in (0, 1):
        sid = span_order[2 * ctx_place + offset]
        piece = lax.dynamic_slice(small, (sid // 2, 0, sid % 2, 0), (1, 4, 1, span))
        pieces.append(piece.reshape(4, span))
    rows = jnp.concatenate(pieces, 1)
    tgt_rows = rows[0].astype(jnp.int32)
    mask_rows, prior_rows, outside = rows[1], rows[2], rows[3]

    def score(tok):
        return lax.dot_general(head, tok, (((1,), (1,)), ((), ())), preferred_element_type=f32)

    mate_part = lax.ppermute(score(mate_half), "core", SWAP)
    logits = score(own_half) + mate_part

    local_col = tgt_rows - block_total - vocab_place * group_rows
    vocab_ids = lax.broadcasted_iota(jnp.int32, (group_rows, tok_rows), 0)
    hits = vocab_ids == local_col[None, :]
    top_local = jnp.max(logits, axis=0)
    sum_local = jnp.sum(jnp.exp(logits - top_local[None, :]), axis=0)
    target_local = jnp.sum(jnp.where(hits, logits, 0.0), axis=0)
    stats = jnp.stack([top_local, sum_local, target_local], 0)
    stats = spread(stats, "vocab", vocab_count)
    top_value = jnp.maximum(prior_rows, jnp.max(stats[:, 0], axis=0))
    sum_total = jnp.sum(stats[:, 1] * jnp.exp(stats[:, 0] - top_value[None, :]), axis=0)
    target_sum = jnp.sum(stats[:, 2], axis=0)
    log_total = top_value + jnp.log(jnp.exp(prior_rows - top_value) + sum_total)
    target_logit = jnp.where(tgt_rows >= block_total, target_sum, outside)
    loss_rows = mask_rows * (log_total - target_logit)
    grad_scale = loss_scale / token_count
    dlogits = (
        mask_rows[None, :]
        * (jnp.exp(logits - log_total[None, :]) - hits.astype(f32))
        * grad_scale
    ).astype(bf16)
    mate_dlogits = lax.ppermute(dlogits, "core", SWAP)

    both = jnp.concatenate([dlogits, mate_dlogits], 1)
    partial_rows = jnp.dot(both, tokens, preferred_element_type=f32).astype(bf16)
    by_y = exchange(partial_rows.reshape(NY, y_rows, half), "y")
    by_y = jnp.sum(by_y.astype(f32), axis=0).astype(bf16)
    by_z = exchange(by_y.reshape(NZ, chip_rows, half), "z")
    chip_grad = jnp.sum(by_z.astype(f32), axis=0)
    square = jnp.sum(chip_grad * chip_grad)
    squares = spread(jnp.full((1, 128), square), ALL, ctx_count * vocab_count)
    square_sum = jnp.sum(squares) / 128.0
    near = lax.dynamic_slice_in_dim(chip_grad, core * shard_rows, shard_rows, 0)
    far = lax.dynamic_slice_in_dim(chip_grad, (1 - core) * shard_rows, shard_rows, 0)
    mate = lax.ppermute(far, "core", SWAP)
    row_grad = jnp.where(
        core == 0, jnp.concatenate([near, mate], 1), jnp.concatenate([mate, near], 1)
    )

    mate_head = lax.ppermute(head, "core", SWAP)
    low = jnp.where(core == 0, head, mate_head)
    high = jnp.where(core == 0, mate_head, head)
    width = feat // vocab_count
    parts = []
    for q in range(vocab_count):
        side = low if q < vocab_count // 2 else high
        at = (q % (vocab_count // 2)) * width
        parts.append(
            lax.dot_general(
                dlogits,
                side[:, at : at + width],
                (((0,), (0,)), ((), ())),
                preferred_element_type=f32,
            ).astype(bf16)
        )
    hidden_parts = exchange(jnp.stack(parts, 0), "vocab")
    hidden_grad = jnp.sum(hidden_parts.astype(f32), axis=0).astype(bf16)

    losses = spread(loss_rows.reshape(2, span), CTX, ctx_count).reshape(2 * ctx_count, span)
    mean_loss = jnp.sum(losses) / token_count
    slot_ids = jnp.arange(span_order.shape[0], dtype=jnp.int32)
    natural = []
    for offset in (0, 1):
        slot = jnp.sum(jnp.where(span_order == 2 * ctx_place + offset, slot_ids, 0))
        natural.append(lax.dynamic_slice_in_dim(losses, slot, 1, 0).reshape(span))
    token_loss = jnp.concatenate(natural, 0)

    norm_value = jnp.sqrt(square_sum) / loss_scale
    clip_factor = jnp.minimum(1.0, clip_norm / (norm_value + 1e-06))
    clipped = row_grad * clip_factor
    new_moment = beta_one * moment + (1.0 - beta_one) * clipped
    new_second = beta_two * second + (1.0 - beta_two) * clipped * clipped
    new_master = master - learn_rate * (
        new_moment / (jnp.sqrt(new_second) + adam_eps) + weight_decay * master
    )
    return (token_loss, mean_loss, hidden_grad, new_master, new_moment, new_second)


def solution(mesh):
    grid = Mesh(mesh.devices.reshape(NY, NZ, NC, mesh.devices.shape[1]), ALL)
    head_spec = P(("vocab",) + CTX, None)
    in_specs = (
        P(CTX, None),
        head_spec,
        head_spec,
        head_spec,
        P(CTX),
        P(CTX),
        P(CTX),
        P(CTX),
        P(),
    )
    out_specs = (P(CTX), P(), P(CTX, "vocab"), head_spec, head_spec, head_spec)
    return jax.shard_map(body, mesh=grid, in_specs=in_specs, out_specs=out_specs, check_vma=False)
```

```python
import jax
import jax.numpy as jnp
from jax import lax
from jax.sharding import Mesh, PartitionSpec as P

loss_scale = 1048576.0
clip_norm = 0.004
beta_one = 0.9
beta_two = 0.95
learn_rate = 0.001
weight_decay = 0.1
adam_eps = 1e-08

NY, NZ, NC = 4, 8, 2
CTX = ("y", "z", "core")
ALL = ("y", "z", "core", "vocab")
SWAP = [(0, 1), (1, 0)]
f32 = jnp.float32
bf16 = jnp.bfloat16


def exchange(x, axes):
    return lax.all_to_all(x, axes, 0, 0, tiled=True)


def shift(x, axis, count, step):
    return lax.ppermute(x, axis, [(i, (i + step) % count) for i in range(count)])


def spread(x, axes, count):
    return exchange(jnp.broadcast_to(x[None], (count,) + x.shape), axes)


def body(
    hidden_states, master, moment, second, targets, loss_mask, prior_lse, prior_target, span_order
):
    tok_rows, feat = hidden_states.shape
    shard_rows = master.shape[0]
    vocab_count = lax.axis_size("vocab")
    ctx_count = NY * NZ * NC
    core = lax.axis_index("core")
    y_place = lax.axis_index("y")
    vocab_place = lax.axis_index("vocab")
    ctx_place = (y_place * NZ + lax.axis_index("z")) * NC + core
    span = tok_rows // 2
    half = feat // 2
    group_rows = shard_rows * ctx_count
    block_total = group_rows * vocab_count
    y_rows = group_rows // NY
    chip_rows = y_rows // NZ

    cut = master.astype(bf16).reshape(shard_rows, NC, half).transpose(1, 0, 2)
    cut = jnp.broadcast_to(cut[None], (NZ,) + cut.shape).reshape(NZ * NC, shard_rows, half)
    block = exchange(cut, ("z", "core")).reshape(y_rows, half)
    head = jnp.concatenate([block] + [shift(block, "y", NY, s) for s in range(1, NY)], 0)

    own_half = lax.dynamic_slice_in_dim(hidden_states, core * half, half, 1)
    far_half = lax.dynamic_slice_in_dim(hidden_states, (1 - core) * half, half, 1)
    mate_half = lax.ppermute(far_half, "core", SWAP)
    tokens = jnp.concatenate([own_half, mate_half], 0)

    small = jnp.concatenate(
        [
            targets.astype(f32).reshape(2, span),
            loss_mask.astype(f32).reshape(2, span),
            prior_lse.reshape(2, span),
            prior_target.reshape(2, span),
        ],
        0,
    )
    small = spread(small, CTX, ctx_count).reshape(ctx_count, 4, 2, span)
    token_count = jnp.sum(small[:, 1])
    pieces = []
    for offset in (0, 1):
        sid = span_order[2 * ctx_place + offset]
        piece = lax.dynamic_slice(small, (sid // 2, 0, sid % 2, 0), (1, 4, 1, span))
        pieces.append(piece.reshape(4, span))
    rows = jnp.concatenate(pieces, 1)
    tgt_rows = rows[0].astype(jnp.int32)
    mask_rows, prior_rows, outside = rows[1], rows[2], rows[3]

    def score(tok):
        return lax.dot_general(head, tok, (((1,), (1,)), ((), ())), preferred_element_type=f32)

    mate_part = lax.ppermute(score(mate_half), "core", SWAP)
    logits = score(own_half) + mate_part

    local_col = tgt_rows - block_total - vocab_place * group_rows
    vocab_ids = lax.broadcasted_iota(jnp.int32, (group_rows, tok_rows), 0)
    vocab_ids = (y_place * y_rows - vocab_ids // y_rows * y_rows) % group_rows + vocab_ids % y_rows
    hits = vocab_ids == local_col[None, :]
    top_local = jnp.max(logits, axis=0)
    sum_local = jnp.sum(jnp.exp(logits - top_local[None, :]), axis=0)
    target_local = jnp.sum(jnp.where(hits, logits, 0.0), axis=0)
    stats = jnp.stack([top_local, sum_local, target_local], 0)
    heard = [stats] + [shift(stats, "vocab", vocab_count, s) for s in range(1, vocab_count)]
    ordered = []
    for j in range(vocab_count):
        back = (vocab_place - j) % vocab_count
        pick = heard[0]
        for s in range(1, vocab_count):
            pick = jnp.where(back == s, heard[s], pick)
        ordered.append(pick)
    stats = jnp.stack(ordered, 0)
    top_value = jnp.maximum(prior_rows, jnp.max(stats[:, 0], axis=0))
    sum_total = jnp.sum(stats[:, 1] * jnp.exp(stats[:, 0] - top_value[None, :]), axis=0)
    target_sum = jnp.sum(stats[:, 2], axis=0)
    log_total = top_value + jnp.log(jnp.exp(prior_rows - top_value) + sum_total)
    target_logit = jnp.where(tgt_rows >= block_total, target_sum, outside)
    loss_rows = mask_rows * (log_total - target_logit)
    grad_scale = loss_scale / token_count
    dlogits = (
        mask_rows[None, :]
        * (jnp.exp(logits - log_total[None, :]) - hits.astype(f32))
        * grad_scale
    ).astype(bf16)
    mate_dlogits = lax.ppermute(dlogits, "core", SWAP)

    both = jnp.concatenate([dlogits, mate_dlogits], 1)
    partial_rows = jnp.dot(both, tokens, preferred_element_type=f32).astype(bf16)
    blocks = [partial_rows[s * y_rows : (s + 1) * y_rows] for s in range(NY)]
    by_y = blocks[0].astype(f32)
    for s in range(1, NY):
        by_y = by_y + shift(blocks[s], "y", NY, -s).astype(f32)
    by_y = by_y.astype(bf16)
    by_z = exchange(by_y.reshape(NZ, chip_rows, half), "z")
    chip_grad = jnp.sum(by_z.astype(f32), axis=0)
    square = jnp.sum(chip_grad * chip_grad)
    squares = spread(jnp.full((1, 128), square), ALL, ctx_count * vocab_count)
    square_sum = jnp.sum(squares) / 128.0
    near = lax.dynamic_slice_in_dim(chip_grad, core * shard_rows, shard_rows, 0)
    far = lax.dynamic_slice_in_dim(chip_grad, (1 - core) * shard_rows, shard_rows, 0)
    mate = lax.ppermute(far, "core", SWAP)
    row_grad = jnp.where(
        core == 0, jnp.concatenate([near, mate], 1), jnp.concatenate([mate, near], 1)
    )

    mate_head = lax.ppermute(head, "core", SWAP)
    width = feat // vocab_count
    per_half = vocab_count // NC
    hidden_sum = jnp.zeros((tok_rows, width), f32)
    for s in range(vocab_count - 1, -1, -1):
        q = (vocab_place + s) % vocab_count
        at = (q % per_half) * width
        side = jnp.where(
            q // per_half == core,
            lax.dynamic_slice_in_dim(head, at, width, 1),
            lax.dynamic_slice_in_dim(mate_head, at, width, 1),
        )
        part = lax.dot_general(
            dlogits, side, (((0,), (0,)), ((), ())), preferred_element_type=f32
        ).astype(bf16)
        if s:
            part = shift(part, "vocab", vocab_count, s)
        hidden_sum = hidden_sum + part.astype(f32)
    hidden_grad = hidden_sum.astype(bf16)

    losses = spread(loss_rows.reshape(2, span), CTX, ctx_count).reshape(2 * ctx_count, span)
    mean_loss = jnp.sum(losses) / token_count
    slot_ids = jnp.arange(span_order.shape[0], dtype=jnp.int32)
    natural = []
    for offset in (0, 1):
        slot = jnp.sum(jnp.where(span_order == 2 * ctx_place + offset, slot_ids, 0))
        natural.append(lax.dynamic_slice_in_dim(losses, slot, 1, 0).reshape(span))
    token_loss = jnp.concatenate(natural, 0)

    norm_value = jnp.sqrt(square_sum) / loss_scale
    clip_factor = jnp.minimum(1.0, clip_norm / (norm_value + 1e-06))
    clipped = row_grad * clip_factor
    new_moment = beta_one * moment + (1.0 - beta_one) * clipped
    new_second = beta_two * second + (1.0 - beta_two) * clipped * clipped
    new_master = master - learn_rate * (
        new_moment / (jnp.sqrt(new_second) + adam_eps) + weight_decay * master
    )
    return (token_loss, mean_loss, hidden_grad, new_master, new_moment, new_second)


def solution(mesh):
    grid = Mesh(mesh.devices.reshape(NY, NZ, NC, mesh.devices.shape[1]), ALL)
    head_spec = P(("vocab",) + CTX, None)
    in_specs = (
        P(CTX, None),
        head_spec,
        head_spec,
        head_spec,
        P(CTX),
        P(CTX),
        P(CTX),
        P(CTX),
        P(),
    )
    out_specs = (P(CTX), P(), P(CTX, "vocab"), head_spec, head_spec, head_spec)
    return jax.shard_map(body, mesh=grid, in_specs=in_specs, out_specs=out_specs, check_vma=False)
```

```python
import jax
import jax.numpy as jnp
from jax import lax
from jax.sharding import Mesh, PartitionSpec as P


loss_scale = 1048576.0
clip_norm = 0.004
beta_one = 0.9
beta_two = 0.95
learn_rate = 0.001
weight_decay = 0.1
adam_eps = 1e-08

NY, NZ, NC = 4, 8, 2
CTX = ("y", "z", "core")
ALL = ("y", "z", "core", "vocab")
SWAP = [(0, 1), (1, 0)]
f32 = jnp.float32
bf16 = jnp.bfloat16


def exchange(x, axes):
    return lax.all_to_all(x, axes, 0, 0, tiled=True)


def shift(x, axis, count, step):
    return lax.ppermute(x, axis, [(i, (i + step) % count) for i in range(count)])


def pair(x, y, keep, axis):
    return jnp.where(keep, jnp.concatenate([x, y], axis), jnp.concatenate([y, x], axis))


def gather(x):
    x = x[None]
    for axis, count in (("core", NC), ("z", NZ), ("y", NY)):
        place, bit = lax.axis_index(axis), 1
        while bit < count:
            other = lax.ppermute(x, axis, [(i, i ^ bit) for i in range(count)])
            x = pair(x, other, place & bit == 0, 0)
            bit *= 2
    return x


def spread(x, axes, count):
    return exchange(jnp.broadcast_to(x[None], (count,) + x.shape), axes)


def step(
    hidden_states, master, moment, second, targets, loss_mask, prior_lse, prior_target, span_order
):
    tok_rows, feat = hidden_states.shape
    shard_rows = master.shape[0]
    vocab_count = lax.axis_size("vocab")
    ctx_count = NY * NZ * NC
    core = lax.axis_index("core")
    y_place = lax.axis_index("y")
    vocab_place = lax.axis_index("vocab")
    ctx_place = (y_place * NZ + lax.axis_index("z")) * NC + core
    span = tok_rows // 2
    half = feat // 2
    group_rows = shard_rows * ctx_count
    block_total = group_rows * vocab_count
    y_rows = group_rows // NY
    chip_rows = y_rows // NZ

    wide = half * 3 // 4
    thin = half - wide
    halves = master.astype(bf16).reshape(shard_rows, NC, half)
    cut = halves[:, :, :wide].transpose(1, 0, 2)
    cut = jnp.broadcast_to(cut[None], (NZ,) + cut.shape).reshape(NZ * NC, shard_rows, wide)
    block = exchange(cut, ("z", "core")).reshape(y_rows, wide)
    near_b = lax.dynamic_index_in_dim(halves[:, :, wide:], core, 1, keepdims=False)
    far_b = lax.dynamic_index_in_dim(halves[:, :, wide:], 1 - core, 1, keepdims=False)
    chip_b = pair(near_b, lax.ppermute(far_b, "core", SWAP), core == 0, 0)
    chips_b = jnp.stack([chip_b] + [shift(chip_b, "y", NY, s) for s in range(1, NY)], 0)
    head_a = jnp.concatenate([block] + [shift(block, "y", NY, s) for s in range(1, NY)], 0)
    head_b = spread(chips_b, "z", NZ).transpose(1, 0, 2, 3).reshape(group_rows, thin)
    head = jnp.concatenate([head_a, head_b], 1)

    own_half = lax.dynamic_slice_in_dim(hidden_states, core * half, half, 1)
    far_half = lax.dynamic_slice_in_dim(hidden_states, (1 - core) * half, half, 1)
    mate_half = lax.ppermute(far_half, "core", SWAP)
    tokens = jnp.concatenate([own_half, mate_half], 0)

    small = jnp.concatenate(
        [
            targets.astype(f32).reshape(2, span),
            loss_mask.astype(f32).reshape(2, span),
            prior_lse.reshape(2, span),
            prior_target.reshape(2, span),
        ],
        0,
    )
    small = gather(small)
    small = small.reshape(ctx_count, 4, 2, span)
    token_count = jnp.sum(small[:, 1])
    pieces = []
    for offset in (0, 1):
        sid = span_order[2 * ctx_place + offset]
        piece = lax.dynamic_slice(small, (sid // 2, 0, sid % 2, 0), (1, 4, 1, span))
        pieces.append(piece.reshape(4, span))
    rows = jnp.concatenate(pieces, 1)
    tgt_rows = rows[0].astype(jnp.int32)
    mask_rows, prior_rows, outside = rows[1], rows[2], rows[3]

    def score(tok):
        return lax.dot_general(head, tok, (((1,), (1,)), ((), ())), preferred_element_type=f32)

    mate_part = lax.ppermute(score(mate_half), "core", SWAP)
    logits = score(own_half) + mate_part

    local_col = tgt_rows - block_total - vocab_place * group_rows
    vocab_ids = lax.broadcasted_iota(jnp.int32, (group_rows, tok_rows), 0)
    vocab_ids = (y_place * y_rows - vocab_ids // y_rows * y_rows) % group_rows + vocab_ids % y_rows
    hits = vocab_ids == local_col[None, :]
    top_local = jnp.max(logits, axis=0)
    sum_local = jnp.sum(jnp.exp(logits - top_local[None, :]), axis=0)
    target_local = jnp.sum(jnp.where(hits, logits, 0.0), axis=0)
    stats = jnp.stack([top_local, sum_local, target_local], 0)
    heard = [stats] + [shift(stats, "vocab", vocab_count, s) for s in range(1, vocab_count)]
    ordered = []
    for j in range(vocab_count):
        back = (vocab_place - j) % vocab_count
        pick = heard[0]
        for s in range(1, vocab_count):
            pick = jnp.where(back == s, heard[s], pick)
        ordered.append(pick)
    stats = jnp.stack(ordered, 0)
    top_value = jnp.maximum(prior_rows, jnp.max(stats[:, 0], axis=0))
    sum_total = jnp.sum(stats[:, 1] * jnp.exp(stats[:, 0] - top_value[None, :]), axis=0)
    target_sum = jnp.sum(stats[:, 2], axis=0)
    log_total = top_value + jnp.log(jnp.exp(prior_rows - top_value) + sum_total)
    target_logit = jnp.where(tgt_rows >= block_total, target_sum, outside)
    loss_rows = mask_rows * (log_total - target_logit)
    grad_scale = loss_scale / token_count
    dlogits = (
        mask_rows[None, :]
        * (jnp.exp(logits - log_total[None, :]) - hits.astype(f32))
        * grad_scale
    ).astype(bf16)
    mate_dlogits = lax.ppermute(dlogits, "core", SWAP)

    both = jnp.concatenate([dlogits, mate_dlogits], 1)
    partial_rows = jnp.dot(both, tokens, preferred_element_type=f32).astype(bf16)
    blocks = [partial_rows[s * y_rows : (s + 1) * y_rows, :wide] for s in range(NY)]
    by_y = blocks[0].astype(f32)
    for s in range(1, NY):
        by_y = by_y + shift(blocks[s], "y", NY, -s).astype(f32)
    by_y = by_y.astype(bf16).reshape(NZ, chip_rows, wide)
    by_z = partial_rows[:, wide:].reshape(NY, NZ, chip_rows, thin).transpose(1, 0, 2, 3)
    by_z = jnp.sum(exchange(by_z, "z").astype(f32), axis=0).astype(bf16)
    grad_b = by_z[0].astype(f32)
    for s in range(1, NY):
        grad_b = grad_b + shift(by_z[s], "y", NY, -s).astype(f32)
    grad_a = jnp.sum(exchange(by_y, "z").astype(f32), axis=0)
    chip_grad = jnp.concatenate([grad_a, grad_b], 1)
    square = jnp.sum(chip_grad * chip_grad)
    lanes = tok_rows // vocab_count
    share = lax.dynamic_slice_in_dim(loss_rows, vocab_place * lanes, lanes, 0)
    report = jnp.concatenate([jnp.full((lanes,), square), share], 0)[None]
    reports = spread(report, ALL, ctx_count * vocab_count)[:, 0]
    square_sum = jnp.sum(reports[:, :lanes]) / lanes
    mean_loss = jnp.sum(reports[:, lanes:]) / token_count
    near = lax.dynamic_slice_in_dim(chip_grad, core * shard_rows, shard_rows, 0)
    far = lax.dynamic_slice_in_dim(chip_grad, (1 - core) * shard_rows, shard_rows, 0)
    mate = lax.ppermute(far, "core", SWAP)
    row_grad = jnp.where(
        core == 0, jnp.concatenate([near, mate], 1), jnp.concatenate([mate, near], 1)
    )

    mate_head = lax.ppermute(head, "core", SWAP)
    width = feat // vocab_count
    per_half = vocab_count // NC
    hidden_sum = jnp.zeros((tok_rows, width), f32)
    for s in range(vocab_count - 1, -1, -1):
        q = (vocab_place + s) % vocab_count
        at = (q % per_half) * width
        side = jnp.where(
            q // per_half == core,
            lax.dynamic_slice_in_dim(head, at, width, 1),
            lax.dynamic_slice_in_dim(mate_head, at, width, 1),
        )
        part = lax.dot_general(
            dlogits, side, (((0,), (0,)), ((), ())), preferred_element_type=f32
        ).astype(bf16)
        if s:
            part = shift(part, "vocab", vocab_count, s)
        hidden_sum = hidden_sum + part.astype(f32)
    hidden_grad = hidden_sum.astype(bf16)

    per_span = vocab_count // 2
    slot_ids = jnp.arange(span_order.shape[0], dtype=jnp.int32)
    natural = []
    for offset in (0, 1):
        slot = jnp.sum(jnp.where(span_order == 2 * ctx_place + offset, slot_ids, 0))
        natural.append(
            lax.dynamic_slice(reports, (slot * per_span, lanes), (per_span, lanes)).reshape(span)
        )
    token_loss = jnp.concatenate(natural, 0)

    norm_value = jnp.sqrt(square_sum) / loss_scale
    clip_factor = jnp.minimum(1.0, clip_norm / (norm_value + 1e-06))
    clipped = row_grad * clip_factor
    new_moment = beta_one * moment + (1.0 - beta_one) * clipped
    new_second = beta_two * second + (1.0 - beta_two) * clipped * clipped
    new_master = master - learn_rate * (
        new_moment / (jnp.sqrt(new_second) + adam_eps) + weight_decay * master
    )
    return (token_loss, mean_loss, hidden_grad, new_master, new_moment, new_second)


def solution(mesh):
    grid = Mesh(mesh.devices.reshape(NY, NZ, NC, mesh.devices.shape[1]), ALL)
    head_spec = P(("vocab",) + CTX, None)
    in_specs = (
        P(CTX, None),
        head_spec,
        head_spec,
        head_spec,
        P(CTX),
        P(CTX),
        P(CTX),
        P(CTX),
        P(),
    )
    out_specs = (P(CTX), P(), P(CTX, "vocab"), head_spec, head_spec, head_spec)
    return jax.shard_map(step, mesh=grid, in_specs=in_specs, out_specs=out_specs, check_vma=False)
```

```python
import jax
import jax.numpy as jnp
from jax import lax
from jax.sharding import Mesh, PartitionSpec as P


loss_scale = 1048576.0
clip_norm = 0.004
beta_one = 0.9
beta_two = 0.95
learn_rate = 0.001
weight_decay = 0.1
adam_eps = 1e-08

NY, NZ, NC = 4, 8, 2
CTX = ("y", "z", "core")
ALL = ("y", "z", "core", "vocab")
SWAP = [(0, 1), (1, 0)]
f32 = jnp.float32
bf16 = jnp.bfloat16


def exchange(x, axes):
    return lax.all_to_all(x, axes, 0, 0, tiled=True)


def shift(x, axis, count, step):
    return lax.ppermute(x, axis, [(i, (i + step) % count) for i in range(count)])


def pair(x, y, keep, axis):
    return jnp.where(keep, jnp.concatenate([x, y], axis), jnp.concatenate([y, x], axis))


def split(x, count):
    out = []
    for _ in range(count):
        out.append(lax.reduce_precision(x, 8, 7))
        x = x - out[-1]
    return out


def spread(x, axes, count):
    return exchange(jnp.broadcast_to(x[None], (count,) + x.shape), axes)


def step(
    hidden_states, master, moment, second, targets, loss_mask, prior_lse, prior_target, span_order
):
    tok_rows, feat = hidden_states.shape
    shard_rows = master.shape[0]
    vocab_count = lax.axis_size("vocab")
    ctx_count = NY * NZ * NC
    core = lax.axis_index("core")
    y_place = lax.axis_index("y")
    vocab_place = lax.axis_index("vocab")
    ctx_place = (y_place * NZ + lax.axis_index("z")) * NC + core
    span = tok_rows // 2
    half = feat // 2
    group_rows = shard_rows * ctx_count
    block_total = group_rows * vocab_count
    y_rows = group_rows // NY
    chip_rows = y_rows // NZ

    thin = half * 3 // 16
    wide = half - thin
    halves = master.astype(bf16).reshape(shard_rows, NC, half)
    cut = halves[:, :, :wide].transpose(1, 0, 2)
    cut = jnp.broadcast_to(cut[None], (NZ,) + cut.shape).reshape(NZ * NC, shard_rows, wide)
    block = exchange(cut, ("z", "core")).reshape(y_rows, wide)
    digit = 256
    pieces = [targets // digit, targets % digit, loss_mask]
    pieces = [p.astype(f32) for p in pieces] + split(prior_lse, 3) + split(prior_target, 2)
    small = jnp.concatenate(
        [jnp.stack(pieces[:4], 0), jnp.stack(pieces[4:], 0)], 1
    ).astype(bf16)
    near_b = lax.dynamic_index_in_dim(halves[:, :, wide:], core, 1, keepdims=False)
    far_b = lax.dynamic_index_in_dim(halves[:, :, wide:], 1 - core, 1, keepdims=False)
    near_b = jnp.concatenate([near_b, small], 1)
    far_b = jnp.concatenate([far_b, small], 1)
    far_b = lax.ppermute(far_b, "core", SWAP)
    chip_b = pair(near_b, far_b, core == 0, 0)
    chips_b = jnp.stack([chip_b] + [shift(chip_b, "y", NY, s) for s in range(1, NY)], 0)
    head_a = jnp.concatenate([block] + [shift(block, "y", NY, s) for s in range(1, NY)], 0)
    part_b = spread(chips_b, "z", NZ)
    head_b = part_b[..., :thin].transpose(1, 0, 2, 3).reshape(group_rows, thin)
    head = jnp.concatenate([head_a, head_b], 1)
    small = part_b[..., thin:]

    own_half = lax.dynamic_slice_in_dim(hidden_states, core * half, half, 1)
    far_half = lax.dynamic_slice_in_dim(hidden_states, (1 - core) * half, half, 1)
    mate_half = lax.ppermute(far_half, "core", SWAP)
    tokens = jnp.concatenate([own_half, mate_half], 0)

    masks = small.reshape(NZ, NY, NC, shard_rows, 2 * tok_rows)[:, :, :, 2, :tok_rows]
    token_count = jnp.sum(masks.astype(f32))
    found = []
    for offset in (0, 1):
        sid = span_order[2 * ctx_place + offset]
        owner = sid // 2
        at_y, at_z, at_core = owner // (NZ * NC), owner // NC % NZ, owner % NC
        start = [at_z, (y_place - at_y) % NY, at_core * shard_rows]
        for side in (0, 1):
            lane = side * tok_rows + sid % 2 * span
            found.append(
                lax.dynamic_slice(small, start + [lane], (1, 1, shard_rows, span)).reshape(
                    shard_rows, span
                )
            )
    rows_a = jnp.concatenate([found[0], found[2]], 1).astype(f32)
    rows_b = jnp.concatenate([found[1], found[3]], 1).astype(f32)
    tgt_rows = (rows_a[0] * digit + rows_a[1]).astype(jnp.int32)
    mask_rows = rows_a[2]
    prior_rows = rows_a[3] + rows_b[0] + rows_b[1]
    outside = rows_b[2] + rows_b[3]

    def score(tok):
        return lax.dot_general(head, tok, (((1,), (1,)), ((), ())), preferred_element_type=f32)

    mate_part = score(mate_half)
    mate_head = lax.ppermute(head, "core", SWAP)
    mate_part = lax.ppermute(mate_part, "core", SWAP)
    logits = score(own_half) + mate_part

    local_col = tgt_rows - block_total - vocab_place * group_rows
    vocab_ids = lax.broadcasted_iota(jnp.int32, (group_rows, tok_rows), 0)
    vocab_ids = (y_place * y_rows - vocab_ids // y_rows * y_rows) % group_rows + vocab_ids % y_rows
    hits = vocab_ids == local_col[None, :]
    top_local = jnp.max(logits, axis=0)
    sum_local = jnp.sum(jnp.exp(logits - top_local[None, :]), axis=0)
    target_local = jnp.sum(jnp.where(hits, logits, 0.0), axis=0)
    stats = jnp.stack([top_local, sum_local, target_local], 0)
    heard = [stats] + [shift(stats, "vocab", vocab_count, s) for s in range(1, vocab_count)]
    ordered = []
    for j in range(vocab_count):
        back = (vocab_place - j) % vocab_count
        pick = heard[0]
        for s in range(1, vocab_count):
            pick = jnp.where(back == s, heard[s], pick)
        ordered.append(pick)
    stats = jnp.stack(ordered, 0)
    top_value = jnp.maximum(prior_rows, jnp.max(stats[:, 0], axis=0))
    sum_total = jnp.sum(stats[:, 1] * jnp.exp(stats[:, 0] - top_value[None, :]), axis=0)
    target_sum = jnp.sum(stats[:, 2], axis=0)
    log_total = top_value + jnp.log(jnp.exp(prior_rows - top_value) + sum_total)
    target_logit = jnp.where(tgt_rows >= block_total, target_sum, outside)
    loss_rows = mask_rows * (log_total - target_logit)
    grad_scale = loss_scale / token_count
    dlogits = (
        mask_rows[None, :]
        * (jnp.exp(logits - log_total[None, :]) - hits.astype(f32))
        * grad_scale
    ).astype(bf16)
    mate_dlogits = lax.ppermute(dlogits, "core", SWAP)

    both = jnp.concatenate([dlogits, mate_dlogits], 1)
    partial_rows = jnp.dot(both, tokens, preferred_element_type=f32).astype(bf16)
    blocks = [partial_rows[s * y_rows : (s + 1) * y_rows, :wide] for s in range(NY)]
    by_y = blocks[0].astype(f32)
    for s in range(1, NY):
        by_y = by_y + shift(blocks[s], "y", NY, -s).astype(f32)
    by_y = by_y.astype(bf16).reshape(NZ, chip_rows, wide)
    by_z = partial_rows[:, wide:].reshape(NY, NZ, chip_rows, thin).transpose(1, 0, 2, 3)
    by_z = jnp.sum(exchange(by_z, "z").astype(f32), axis=0).astype(bf16)
    grad_b = by_z[0].astype(f32)
    for s in range(1, NY):
        grad_b = grad_b + shift(by_z[s], "y", NY, -s).astype(f32)
    grad_a = jnp.sum(exchange(by_y, "z").astype(f32), axis=0)
    chip_grad = jnp.concatenate([grad_a, grad_b], 1)
    square = jnp.sum(chip_grad * chip_grad)
    lanes = tok_rows // vocab_count
    share = lax.dynamic_slice_in_dim(loss_rows, vocab_place * lanes, lanes, 0)
    report = jnp.concatenate([jnp.full((lanes,), square), share], 0)[None]
    reports = spread(report, ALL, ctx_count * vocab_count)[:, 0]
    square_sum = jnp.sum(reports[:, :lanes]) / lanes
    mean_loss = jnp.sum(reports[:, lanes:]) / token_count
    near = lax.dynamic_slice_in_dim(chip_grad, core * shard_rows, shard_rows, 0)
    far = lax.dynamic_slice_in_dim(chip_grad, (1 - core) * shard_rows, shard_rows, 0)
    mate = lax.ppermute(far, "core", SWAP)
    row_grad = jnp.where(
        core == 0, jnp.concatenate([near, mate], 1), jnp.concatenate([mate, near], 1)
    )

    width = feat // vocab_count
    per_half = vocab_count // NC
    hidden_parts = []
    for s in range(vocab_count - 1, -1, -1):
        q = (vocab_place + s) % vocab_count
        at = (q % per_half) * width
        side = jnp.where(
            q // per_half == core,
            lax.dynamic_slice_in_dim(head, at, width, 1),
            lax.dynamic_slice_in_dim(mate_head, at, width, 1),
        )
        side = lax.optimization_barrier(side)
        part = lax.dot_general(
            dlogits, side, (((0,), (0,)), ((), ())), preferred_element_type=f32
        ).astype(bf16)
        if s:
            part = shift(part, "vocab", vocab_count, s)
        hidden_parts.append(part)
    hidden_grad = sum(part.astype(f32) for part in hidden_parts).astype(bf16)

    per_span = vocab_count // 2
    slot_ids = jnp.arange(span_order.shape[0], dtype=jnp.int32)
    natural = []
    for offset in (0, 1):
        slot = jnp.sum(jnp.where(span_order == 2 * ctx_place + offset, slot_ids, 0))
        natural.append(
            lax.dynamic_slice(reports, (slot * per_span, lanes), (per_span, lanes)).reshape(span)
        )
    token_loss = jnp.concatenate(natural, 0)

    norm_value = jnp.sqrt(square_sum) / loss_scale
    clip_factor = jnp.minimum(1.0, clip_norm / (norm_value + 1e-06))
    clipped = row_grad * clip_factor
    new_moment = beta_one * moment + (1.0 - beta_one) * clipped
    new_second = beta_two * second + (1.0 - beta_two) * clipped * clipped
    new_master = master - learn_rate * (
        new_moment / (jnp.sqrt(new_second) + adam_eps) + weight_decay * master
    )
    return (token_loss, mean_loss, hidden_grad, new_master, new_moment, new_second)


def solution(mesh):
    grid = Mesh(mesh.devices.reshape(NY, NZ, NC, mesh.devices.shape[1]), ALL)
    head_spec = P(("vocab",) + CTX, None)
    in_specs = (
        P(CTX, None),
        head_spec,
        head_spec,
        head_spec,
        P(CTX),
        P(CTX),
        P(CTX),
        P(CTX),
        P(),
    )
    out_specs = (P(CTX), P(), P(CTX, "vocab"), head_spec, head_spec, head_spec)
    return jax.shard_map(step, mesh=grid, in_specs=in_specs, out_specs=out_specs, check_vma=False)
```

```python
import jax
import jax.numpy as jnp
from jax import lax
from jax.sharding import Mesh, PartitionSpec as P


loss_scale = 1048576.0
clip_norm = 0.004
beta_one = 0.9
beta_two = 0.95
learn_rate = 0.001
weight_decay = 0.1
adam_eps = 1e-08

NY, NZ, NC = 4, 8, 2
CTX = ("y", "z", "core")
ALL = ("y", "z", "core", "vocab")
SWAP = [(0, 1), (1, 0)]
f32 = jnp.float32
bf16 = jnp.bfloat16


def exchange(x, axes):
    return lax.all_to_all(x, axes, 0, 0, tiled=True)


def shift(x, axis, count, step):
    return lax.ppermute(x, axis, [(i, (i + step) % count) for i in range(count)])


def pair(x, y, keep, axis):
    return jnp.where(keep, jnp.concatenate([x, y], axis), jnp.concatenate([y, x], axis))


def split(x, count):
    out = []
    for _ in range(count):
        out.append(lax.reduce_precision(x, 8, 7))
        x = x - out[-1]
    return out


def spread(x, axes, count):
    return exchange(jnp.broadcast_to(x[None], (count,) + x.shape), axes)


def step(
    hidden_states, master, moment, second, targets, loss_mask, prior_lse, prior_target, span_order
):
    tok_rows, feat = hidden_states.shape
    shard_rows = master.shape[0]
    vocab_count = lax.axis_size("vocab")
    ctx_count = NY * NZ * NC
    core = lax.axis_index("core")
    y_place = lax.axis_index("y")
    vocab_place = lax.axis_index("vocab")
    ctx_place = (y_place * NZ + lax.axis_index("z")) * NC + core
    span = tok_rows // 2
    half = feat // 2
    group_rows = shard_rows * ctx_count
    block_total = group_rows * vocab_count
    y_rows = group_rows // NY
    chip_rows = y_rows // NZ

    thin = half // 8
    wide = half - thin
    thin_g = half * 3 // 16
    wide_g = half - thin_g
    halves = master.astype(bf16).reshape(shard_rows, NC, half)
    cut = halves[:, :, :wide].transpose(1, 0, 2)
    cut = jnp.broadcast_to(cut[None], (NZ,) + cut.shape).reshape(NZ * NC, shard_rows, wide)
    block = exchange(cut, ("z", "core")).reshape(y_rows, wide)
    digit = 256
    pieces = [targets // digit, targets % digit, loss_mask]
    pieces = [p.astype(f32) for p in pieces] + split(prior_lse, 3) + split(prior_target, 2)
    small = jnp.concatenate(
        [jnp.stack(pieces[:4], 0), jnp.stack(pieces[4:], 0)], 1
    ).astype(bf16)
    near_b = lax.dynamic_index_in_dim(halves[:, :, wide:], core, 1, keepdims=False)
    far_b = lax.dynamic_index_in_dim(halves[:, :, wide:], 1 - core, 1, keepdims=False)
    near_b = jnp.concatenate([near_b, small], 1)
    far_b = jnp.concatenate([far_b, small], 1)
    far_b = lax.ppermute(far_b, "core", SWAP)
    chip_b = pair(near_b, far_b, core == 0, 0)
    chips_b = jnp.stack([chip_b] + [shift(chip_b, "y", NY, s) for s in range(1, NY)], 0)
    head_a = jnp.concatenate([block] + [shift(block, "y", NY, s) for s in range(1, NY)], 0)
    part_b = spread(chips_b, "z", NZ)
    sids = lax.dynamic_slice(
        span_order, (2 * ctx_place,), (2,), allow_negative_indices=False
    )
    owner = sids >> 1
    starts = [
        (owner >> 1) & (NZ - 1),
        (y_place - (owner >> 4)) & (NY - 1),
        (owner & 1) * shard_rows,
        (sids & 1) * span,
    ]
    starts = lax.optimization_barrier([[v[i] for v in starts] for i in (0, 1)])
    slot_ids = jnp.arange(span_order.shape[0], dtype=jnp.int32)
    slots = [
        jnp.sum(jnp.where(span_order == 2 * ctx_place + offset, slot_ids, 0))
        for offset in (0, 1)
    ]
    slots = lax.optimization_barrier([slot * (vocab_count // 2) for slot in slots])
    head_b = part_b[..., :thin].transpose(1, 0, 2, 3).reshape(group_rows, thin)
    head = jnp.concatenate([head_a, head_b], 1)
    small = part_b[..., thin:]

    own_half = lax.dynamic_slice_in_dim(hidden_states, core * half, half, 1)
    far_half = lax.dynamic_slice_in_dim(hidden_states, (1 - core) * half, half, 1)
    mate_half = lax.ppermute(far_half, "core", SWAP)
    tokens = jnp.concatenate([own_half, mate_half], 0)

    masks = small.reshape(NZ, NY, NC, shard_rows, 2 * tok_rows)[:, :, :, 2, :tok_rows]
    token_count = jnp.sum(masks.astype(f32))
    found = [
        lax.dynamic_slice(
            small,
            (at[0], at[1], at[2], at[3] + side * tok_rows),
            (1, 1, shard_rows, span),
            allow_negative_indices=False,
        ).reshape(shard_rows, span)
        for at in starts
        for side in (0, 1)
    ]
    rows_a = jnp.concatenate([found[0], found[2]], 1).astype(f32)
    rows_b = jnp.concatenate([found[1], found[3]], 1).astype(f32)
    tgt_rows = (rows_a[0] * digit + rows_a[1]).astype(jnp.int32)
    mask_rows = rows_a[2]
    prior_rows = rows_a[3] + rows_b[0] + rows_b[1]
    outside = rows_b[2] + rows_b[3]

    def score(tok):
        return lax.dot_general(head, tok, (((1,), (1,)), ((), ())), preferred_element_type=f32)

    mate_part = score(mate_half)
    mate_head = lax.ppermute(head, "core", SWAP)
    mate_part = lax.ppermute(mate_part, "core", SWAP)
    logits = score(own_half) + mate_part

    local_col = tgt_rows - block_total - vocab_place * group_rows
    vocab_ids = lax.broadcasted_iota(jnp.int32, (group_rows, tok_rows), 0)
    within = vocab_ids & (y_rows - 1)
    vocab_ids = ((y_place * y_rows - (vocab_ids - within)) & (group_rows - 1)) + within
    hits = vocab_ids == local_col[None, :]
    top_local = jnp.max(logits, axis=0)
    sum_local = jnp.sum(jnp.exp(logits - top_local[None, :]), axis=0)
    target_local = jnp.sum(jnp.where(hits, logits, 0.0), axis=0)
    stats = jnp.stack([top_local, sum_local, target_local], 0)
    heard = [stats] + [shift(stats, "vocab", vocab_count, s) for s in range(1, vocab_count)]
    ordered = []
    for j in range(vocab_count):
        back = (vocab_place - j) % vocab_count
        pick = heard[0]
        for s in range(1, vocab_count):
            pick = jnp.where(back == s, heard[s], pick)
        ordered.append(pick)
    stats = jnp.stack(ordered, 0)
    top_value = jnp.maximum(prior_rows, jnp.max(stats[:, 0], axis=0))
    sum_total = jnp.sum(stats[:, 1] * jnp.exp(stats[:, 0] - top_value[None, :]), axis=0)
    target_sum = jnp.sum(stats[:, 2], axis=0)
    log_total = top_value + jnp.log(jnp.exp(prior_rows - top_value) + sum_total)
    target_logit = jnp.where(tgt_rows >= block_total, target_sum, outside)
    loss_rows = mask_rows * (log_total - target_logit)
    grad_scale = loss_scale / token_count
    dlogits = (
        mask_rows[None, :]
        * (jnp.exp(logits - log_total[None, :]) - hits.astype(f32))
        * grad_scale
    ).astype(bf16)
    mate_dlogits = lax.ppermute(dlogits, "core", SWAP)

    both = jnp.concatenate([dlogits, mate_dlogits], 1)
    partial_rows = jnp.dot(both, tokens, preferred_element_type=f32).astype(bf16)
    blocks = [partial_rows[s * y_rows : (s + 1) * y_rows, :wide_g] for s in range(NY)]
    by_y = blocks[0].astype(f32)
    for s in range(1, NY):
        by_y = by_y + shift(blocks[s], "y", NY, -s).astype(f32)
    by_y = by_y.astype(bf16).reshape(NZ, chip_rows, wide_g)
    by_z = partial_rows[:, wide_g:].reshape(NY, NZ, chip_rows, thin_g).transpose(1, 0, 2, 3)
    by_z = jnp.sum(exchange(by_z, "z").astype(f32), axis=0).astype(bf16)
    grad_b = by_z[0].astype(f32)
    for s in range(1, NY):
        grad_b = grad_b + shift(by_z[s], "y", NY, -s).astype(f32)
    grad_a = jnp.sum(exchange(by_y, "z").astype(f32), axis=0)
    chip_grad = jnp.concatenate([grad_a, grad_b], 1)
    square = jnp.sum(chip_grad * chip_grad)
    lanes = tok_rows // vocab_count
    share = lax.dynamic_slice_in_dim(loss_rows, vocab_place * lanes, lanes, 0)
    share = jnp.pad(share, (0, span - lanes))
    report = jnp.concatenate([jnp.full((1, span), square), share[None]], 0)
    reports = spread(report, ALL, ctx_count * vocab_count)
    square_sum = jnp.sum(reports[:, 0], axis=0)
    mean_loss = jnp.sum(reports[:, 1]) * (1.0 / token_count)
    near = lax.dynamic_slice_in_dim(chip_grad, core * shard_rows, shard_rows, 0)
    far = lax.dynamic_slice_in_dim(chip_grad, (1 - core) * shard_rows, shard_rows, 0)
    mate = lax.ppermute(far, "core", SWAP)
    row_grad = jnp.where(
        core == 0, jnp.concatenate([near, mate], 1), jnp.concatenate([mate, near], 1)
    )

    width = feat // vocab_count
    per_half = vocab_count // NC
    hidden_parts = []
    for s in range(vocab_count - 1, -1, -1):
        q = (vocab_place + s) & (vocab_count - 1)
        at = (q & (per_half - 1)) * width
        side = jnp.where(
            (q >= per_half) == (core == 1),
            lax.dynamic_slice(head, (0, at), (group_rows, width), allow_negative_indices=False),
            lax.dynamic_slice(
                mate_head, (0, at), (group_rows, width), allow_negative_indices=False
            ),
        )
        if s == 2:
            side = lax.optimization_barrier(side)
        part = lax.dot_general(
            dlogits, side, (((0,), (0,)), ((), ())), preferred_element_type=f32
        ).astype(bf16)
        if s:
            part = shift(part, "vocab", vocab_count, s)
        else:
            part = lax.optimization_barrier(part)
        hidden_parts.append(part)
    hidden_grad = sum(part.astype(f32) for part in hidden_parts).astype(bf16)

    per_span = vocab_count // 2
    natural = [
        lax.dynamic_slice(
            reports, (slot, 1, 0), (per_span, 1, lanes), allow_negative_indices=False
        ).reshape(span)
        for slot in slots
    ]
    token_loss = jnp.concatenate(natural, 0)

    norm_value = jnp.sqrt(square_sum) / loss_scale
    clip_factor = jnp.minimum(1.0, clip_norm / (norm_value + 1e-06))
    clip_factor = jnp.broadcast_to(clip_factor, (shard_rows, feat // span, span))
    clipped = row_grad * clip_factor.reshape(shard_rows, feat)
    new_moment = beta_one * moment + (1.0 - beta_one) * clipped
    new_second = beta_two * second + (1.0 - beta_two) * clipped * clipped
    new_master = master - learn_rate * (
        new_moment / (jnp.sqrt(new_second) + adam_eps) + weight_decay * master
    )
    return (token_loss, mean_loss, hidden_grad, new_master, new_moment, new_second)


def solution(mesh):
    grid = Mesh(mesh.devices.reshape(NY, NZ, NC, mesh.devices.shape[1]), ALL)
    head_spec = P(("vocab",) + CTX, None)
    in_specs = (
        P(CTX, None),
        head_spec,
        head_spec,
        head_spec,
        P(CTX),
        P(CTX),
        P(CTX),
        P(CTX),
        P(),
    )
    out_specs = (P(CTX), P(), P(CTX, "vocab"), head_spec, head_spec, head_spec)
    return jax.shard_map(step, mesh=grid, in_specs=in_specs, out_specs=out_specs, check_vma=False)
```

```python
import functools

import jax
import jax.numpy as jnp
from jax import lax
from jax.experimental import pallas as pl
from jax.experimental.pallas import tpu as pltpu
from jax.sharding import Mesh, PartitionSpec as P


loss_scale = 1048576.0
clip_norm = 0.004
beta_one = 0.9
beta_two = 0.95
learn_rate = 0.001
weight_decay = 0.1
adam_eps = 1e-08

NY, NZ, NC = 4, 8, 2
CTX = ("y", "z", "core")
ALL = ("y", "z", "core", "vocab")
SWAP = [(0, 1), (1, 0)]
f32 = jnp.float32
bf16 = jnp.bfloat16


def exchange(x, axes):
    return lax.all_to_all(x, axes, 0, 0, tiled=True)


def shift(x, axis, count, step):
    return lax.ppermute(x, axis, [(i, (i + step) % count) for i in range(count)])


def pair(x, y, keep, axis):
    return jnp.where(keep, jnp.concatenate([x, y], axis), jnp.concatenate([y, x], axis))


def split(x, count):
    out = []
    for _ in range(count):
        out.append(lax.reduce_precision(x, 8, 7))
        x = x - out[-1]
    return out


def spread(x, axes, count):
    return exchange(jnp.broadcast_to(x[None], (count,) + x.shape), axes)


def front_kernel(
    group, y_rows, span_ref, place_ref, small_ref, own_ref, mate_ref, logit_ref, stat_ref, row_ref
):
    ctx, y_place, vocab_place = place_ref[0], place_ref[1], place_ref[2]
    tok = own_ref.shape[1]
    span = tok // 2
    quads = small_ref.shape[2] // NC
    left, right = [], []
    for offset in (0, 1):
        sid = span_ref[2 * ctx + offset]
        at_z = (sid >> 2) & (NZ - 1)
        at_y = (y_place - (sid >> 5)) & (NY - 1)
        chip = small_ref[at_z, at_y].astype(f32)
        mine = jnp.where((sid & 2) == 0, chip[:quads], chip[quads:])
        odd = (sid & 1) == 1
        left.append(jnp.where(odd, mine[:, span:tok], mine[:, :span]))
        right.append(jnp.where(odd, mine[:, tok + span :], mine[:, tok : tok + span]))
    left = jnp.concatenate(left, 1)
    right = jnp.concatenate(right, 1)
    marks = jnp.sum(small_ref[:, :, :, :tok].astype(f32), axis=(0, 1))
    marks = marks[2:3] + marks[quads + 2 : quads + 3]
    token_count = jnp.sum(marks, axis=1, keepdims=True)
    target = left[0:1] * 256.0 + left[1:2]
    mask = left[2:3]
    local = target.astype(jnp.int32) - group * 4 - vocab_place * group
    ids = lax.broadcasted_iota(jnp.int32, (group, tok), 0)
    within = ids & (y_rows - 1)
    ids = ((y_place * y_rows - (ids - within)) & (group - 1)) + within
    hits = ids == local
    logits = own_ref[...] + mate_ref[...]
    logit_ref[...] = logits
    top = jnp.max(logits, axis=0, keepdims=True)
    stat_ref[0:1, :] = top
    stat_ref[1:2, :] = jnp.sum(jnp.exp(logits - top), axis=0, keepdims=True)
    stat_ref[2:3, :] = jnp.sum(jnp.where(hits, logits, 0.0), axis=0, keepdims=True)
    stat_ref[3:8, :] = jnp.zeros((5, tok), f32)
    row_ref[0:1, :] = target
    row_ref[1:2, :] = mask
    row_ref[2:3, :] = left[3:4] + right[0:1] + right[1:2]
    row_ref[3:4, :] = right[2:3] + right[3:4]
    row_ref[4:5, :] = mask * (loss_scale / token_count)
    row_ref[5:6, :] = jnp.broadcast_to(1.0 / token_count, (1, tok))
    row_ref[6:8, :] = jnp.zeros((2, tok), f32)


def square_kernel(a_ref, b0_ref, b1_ref, b2_ref, b3_ref, share_ref, grad_ref, report_ref):
    wide = a_ref.shape[2]
    part_a = a_ref[0].astype(f32)
    for i in range(1, a_ref.shape[0]):
        part_a = part_a + a_ref[i].astype(f32)
    part_b = b0_ref[...].astype(f32) + b1_ref[...].astype(f32)
    part_b = part_b + b2_ref[...].astype(f32) + b3_ref[...].astype(f32)
    grad_ref[:, :wide] = part_a
    grad_ref[:, wide:] = part_b
    total = jnp.sum(part_a * part_a, axis=1, keepdims=True)
    total = total + jnp.sum(part_b * part_b, axis=1, keepdims=True)
    total = jnp.sum(total, axis=0, keepdims=True)
    row = jnp.concatenate([jnp.broadcast_to(total, (1, 128)), share_ref[...]], 0)
    report_ref[...] = jnp.broadcast_to(row[None], report_ref.shape)


VMEM = pl.BlockSpec(memory_space=pltpu.VMEM)
SMEM = pl.BlockSpec(memory_space=pltpu.SMEM)


def step(
    hidden_states, master, moment, second, targets, loss_mask, prior_lse, prior_target, span_order
):
    tok_rows, feat = hidden_states.shape
    shard_rows = master.shape[0]
    vocab_count = lax.axis_size("vocab")
    ctx_count = NY * NZ * NC
    core = lax.axis_index("core")
    y_place = lax.axis_index("y")
    vocab_place = lax.axis_index("vocab")
    ctx_place = (y_place * NZ + lax.axis_index("z")) * NC + core
    span = tok_rows // 2
    half = feat // 2
    group_rows = shard_rows * ctx_count
    block_total = group_rows * vocab_count
    y_rows = group_rows // NY
    chip_rows = y_rows // NZ

    thin = half // 8
    wide = half - thin
    thin_g = half * 3 // 16
    wide_g = half - thin_g
    halves = master.astype(bf16).reshape(shard_rows, NC, half)
    cut = halves[:, :, :wide].transpose(1, 0, 2)
    cut = jnp.broadcast_to(cut[None], (NZ,) + cut.shape).reshape(NZ * NC, shard_rows, wide)
    block = exchange(cut, ("z", "core")).reshape(y_rows, wide)
    digit = 256
    pieces = [targets // digit, targets % digit, loss_mask]
    pieces = [p.astype(f32) for p in pieces] + split(prior_lse, 3) + split(prior_target, 2)
    small = jnp.concatenate(
        [jnp.stack(pieces[:4], 0), jnp.stack(pieces[4:], 0)], 1
    ).astype(bf16)
    near_b = lax.dynamic_index_in_dim(halves[:, :, wide:], core, 1, keepdims=False)
    far_b = lax.dynamic_index_in_dim(halves[:, :, wide:], 1 - core, 1, keepdims=False)
    near_b = jnp.concatenate([near_b, small], 1)
    far_b = jnp.concatenate([far_b, small], 1)
    far_b = lax.ppermute(far_b, "core", SWAP)
    chip_b = pair(near_b, far_b, core == 0, 0)
    chips_b = jnp.stack([chip_b] + [shift(chip_b, "y", NY, s) for s in range(1, NY)], 0)
    head_a = jnp.concatenate([block] + [shift(block, "y", NY, s) for s in range(1, NY)], 0)
    part_b = spread(chips_b, "z", NZ)
    slot_ids = jnp.arange(span_order.shape[0], dtype=jnp.int32)
    slots = [
        jnp.sum(jnp.where(span_order == 2 * ctx_place + offset, slot_ids, 0))
        for offset in (0, 1)
    ]
    slots = lax.optimization_barrier([slot * (vocab_count // 2) for slot in slots])
    head_b = part_b[..., :thin].transpose(1, 0, 2, 3).reshape(group_rows, thin)
    head = jnp.concatenate([head_a, head_b], 1)
    small = part_b[..., thin:]

    own_half = lax.dynamic_slice(
        hidden_states, (0, core * half), (tok_rows, half), allow_negative_indices=False
    )
    far_half = lax.dynamic_slice(
        hidden_states, (0, (1 - core) * half), (tok_rows, half), allow_negative_indices=False
    )
    mate_half = lax.ppermute(far_half, "core", SWAP)
    tokens = jnp.concatenate([own_half, mate_half], 0)

    def score(tok):
        return lax.dot_general(head, tok, (((1,), (1,)), ((), ())), preferred_element_type=f32)

    mate_part = score(mate_half)
    mate_head = lax.ppermute(head, "core", SWAP)
    mate_part = lax.ppermute(mate_part, "core", SWAP)
    own_part = score(own_half)
    place = jnp.stack([ctx_place, y_place, vocab_place])
    logits, stats, rows = pl.pallas_call(
        functools.partial(front_kernel, group_rows, y_rows),
        out_shape=(
            jax.ShapeDtypeStruct((group_rows, tok_rows), f32),
            jax.ShapeDtypeStruct((8, tok_rows), f32),
            jax.ShapeDtypeStruct((8, tok_rows), f32),
        ),
        in_specs=[SMEM, SMEM, VMEM, VMEM, VMEM],
        out_specs=(VMEM, VMEM, VMEM),
        name="front",
    )(span_order, place, small, own_part, mate_part)
    tgt_rows = rows[0].astype(jnp.int32)
    mask_rows, prior_rows, outside, mask_scale = rows[1], rows[2], rows[3], rows[4]
    local_col = tgt_rows - block_total - vocab_place * group_rows
    vocab_ids = lax.broadcasted_iota(jnp.int32, (group_rows, tok_rows), 0)
    within = vocab_ids & (y_rows - 1)
    vocab_ids = ((y_place * y_rows - (vocab_ids - within)) & (group_rows - 1)) + within
    hits = vocab_ids == local_col[None, :]
    heard = [stats] + [shift(stats, "vocab", vocab_count, s) for s in range(1, vocab_count)]
    ordered = []
    for j in range(vocab_count):
        back = (vocab_place - j) % vocab_count
        pick = heard[0]
        for s in range(1, vocab_count):
            pick = jnp.where(back == s, heard[s], pick)
        ordered.append(pick)
    stats = jnp.stack(ordered, 0)
    top_value = jnp.maximum(prior_rows, jnp.max(stats[:, 0], axis=0))
    sum_total = jnp.sum(stats[:, 1] * jnp.exp(stats[:, 0] - top_value[None, :]), axis=0)
    target_sum = jnp.sum(stats[:, 2], axis=0)
    log_total = top_value + jnp.log(jnp.exp(prior_rows - top_value) + sum_total)
    target_logit = jnp.where(tgt_rows >= block_total, target_sum, outside)
    loss_rows = mask_rows * (log_total - target_logit)
    dlogits = (
        mask_scale[None, :] * (jnp.exp(logits - log_total[None, :]) - hits.astype(f32))
    ).astype(bf16)
    mate_dlogits = lax.ppermute(dlogits, "core", SWAP)

    both = jnp.concatenate([dlogits, mate_dlogits], 1)
    partial_rows = jnp.dot(both, tokens, preferred_element_type=f32).astype(bf16)
    blocks = [partial_rows[s * y_rows : (s + 1) * y_rows, :wide_g] for s in range(NY)]
    by_y = blocks[0].astype(f32)
    for s in range(1, NY):
        by_y = by_y + shift(blocks[s], "y", NY, -s).astype(f32)
    by_y = by_y.astype(bf16).reshape(NZ, chip_rows, wide_g)
    by_z = partial_rows[:, wide_g:].reshape(NY, NZ, chip_rows, thin_g).transpose(1, 0, 2, 3)
    by_z = jnp.sum(exchange(by_z, "z").astype(f32), axis=0).astype(bf16)
    pieces_b = [by_z[0]] + [shift(by_z[s], "y", NY, -s) for s in range(1, NY)]
    pieces_a = exchange(by_y, "z")
    lanes = tok_rows // vocab_count
    share = lax.dynamic_slice_in_dim(loss_rows, vocab_place * lanes, lanes, 0)
    share = jnp.pad(share, (0, span - lanes))[None]
    chip_grad, report = pl.pallas_call(
        square_kernel,
        out_shape=(
            jax.ShapeDtypeStruct((chip_rows, half), f32),
            jax.ShapeDtypeStruct((ctx_count * vocab_count, 2, span), f32),
        ),
        in_specs=[VMEM] * (NY + 2),
        out_specs=(VMEM, VMEM),
        name="square",
    )(pieces_a, *pieces_b, share)
    reports = exchange(report, ALL)
    square_sum = jnp.sum(reports[:, 0], axis=0)
    mean_loss = jnp.sum(reports[:, 1]) * rows[5, 0]
    near = lax.dynamic_slice_in_dim(chip_grad, core * shard_rows, shard_rows, 0)
    far = lax.dynamic_slice_in_dim(chip_grad, (1 - core) * shard_rows, shard_rows, 0)
    mate = lax.ppermute(far, "core", SWAP)
    row_grad = jnp.where(
        core == 0, jnp.concatenate([near, mate], 1), jnp.concatenate([mate, near], 1)
    )

    width = feat // vocab_count
    per_half = vocab_count // NC
    hidden_parts = []
    for s in range(vocab_count - 1, -1, -1):
        q = (vocab_place + s) & (vocab_count - 1)
        at = (q & (per_half - 1)) * width
        side = jnp.where(
            (q >= per_half) == (core == 1),
            lax.dynamic_slice(head, (0, at), (group_rows, width), allow_negative_indices=False),
            lax.dynamic_slice(
                mate_head, (0, at), (group_rows, width), allow_negative_indices=False
            ),
        )
        if s == 2:
            side = lax.optimization_barrier(side)
        part = lax.dot_general(
            dlogits, side, (((0,), (0,)), ((), ())), preferred_element_type=f32
        ).astype(bf16)
        if s:
            part = shift(part, "vocab", vocab_count, s)
        else:
            part = lax.optimization_barrier(part)
        hidden_parts.append(part)
    hidden_grad = sum(part.astype(f32) for part in hidden_parts).astype(bf16)

    per_span = vocab_count // 2
    natural = [
        lax.dynamic_slice(
            reports, (slot, 1, 0), (per_span, 1, lanes), allow_negative_indices=False
        ).reshape(span)
        for slot in slots
    ]
    token_loss = jnp.concatenate(natural, 0)

    norm_value = jnp.sqrt(square_sum) / loss_scale
    clip_factor = jnp.minimum(1.0, clip_norm / (norm_value + 1e-06))
    clip_factor = jnp.broadcast_to(clip_factor, (shard_rows, feat // span, span))
    clipped = row_grad * clip_factor.reshape(shard_rows, feat)
    new_moment = beta_one * moment + (1.0 - beta_one) * clipped
    new_second = beta_two * second + (1.0 - beta_two) * clipped * clipped
    new_master = master - learn_rate * (
        new_moment / (jnp.sqrt(new_second) + adam_eps) + weight_decay * master
    )
    return (token_loss, mean_loss, hidden_grad, new_master, new_moment, new_second)


def solution(mesh):
    grid = Mesh(mesh.devices.reshape(NY, NZ, NC, mesh.devices.shape[1]), ALL)
    head_spec = P(("vocab",) + CTX, None)
    in_specs = (
        P(CTX, None),
        head_spec,
        head_spec,
        head_spec,
        P(CTX),
        P(CTX),
        P(CTX),
        P(CTX),
        P(),
    )
    out_specs = (P(CTX), P(), P(CTX, "vocab"), head_spec, head_spec, head_spec)
    return jax.shard_map(step, mesh=grid, in_specs=in_specs, out_specs=out_specs, check_vma=False)
```

```python
import functools

import jax
import jax.numpy as jnp
from jax import lax
from jax.experimental import pallas as pl
from jax.experimental.pallas import tpu as pltpu
from jax.sharding import Mesh, PartitionSpec as P


loss_scale = 1048576.0
clip_norm = 0.004
beta_one = 0.9
beta_two = 0.95
learn_rate = 0.001
weight_decay = 0.1
adam_eps = 1e-08

NY, NZ, NC = 4, 8, 2
CTX = ("y", "z", "core")
ALL = ("y", "z", "core", "vocab")
SWAP = [(0, 1), (1, 0)]
f32 = jnp.float32
bf16 = jnp.bfloat16


def exchange(x, axes):
    return lax.all_to_all(x, axes, 0, 0, tiled=True)


def shift(x, axis, count, step):
    return lax.ppermute(x, axis, [(i, (i + step) % count) for i in range(count)])


def pair(x, y, keep, axis):
    return jnp.where(keep, jnp.concatenate([x, y], axis), jnp.concatenate([y, x], axis))


def split(x, count):
    out = []
    for _ in range(count):
        out.append(lax.reduce_precision(x, 8, 7))
        x = x - out[-1]
    return out


def spread(x, axes, count):
    return exchange(jnp.broadcast_to(x[None], (count,) + x.shape), axes)


def score_kernel(thin, a0_ref, a1_ref, a2_ref, a3_ref, b_ref, tok_ref, head_ref, part_ref):
    wide = a0_ref.shape[1]
    y_rows = a0_ref.shape[0]
    for s, a_ref in enumerate((a0_ref, a1_ref, a2_ref, a3_ref)):
        head_ref[s * y_rows : (s + 1) * y_rows, :wide] = a_ref[...]
        for z in range(NZ):
            at = s * y_rows + z * (y_rows // NZ)
            head_ref[at : at + y_rows // NZ, wide:] = b_ref[z, s, :, :thin]
    part_ref[...] = lax.dot_general(
        head_ref[...], tok_ref[...], (((1,), (1,)), ((), ())), preferred_element_type=f32
    )


def final_kernel(
    place_ref, report_ref, row_ref, near_ref, mate_ref, master_ref, moment_ref, second_ref,
    loss_ref, mean_ref, new_master_ref, new_moment_ref, new_second_ref,
):
    sums = jnp.sum(report_ref[...], axis=0)
    norm_value = jnp.sqrt(sums[0:1, 0:1]) / loss_scale
    clip_factor = jnp.minimum(1.0, clip_norm / (norm_value + 1e-06))
    lanes = report_ref.shape[2] // 2
    mean_ref[...] = jnp.sum(sums[:, lanes:], axis=1, keepdims=True) * row_ref[5:6, 0:1]
    for i in (0, 1):
        slot = place_ref[3 + i]
        for j in (0, 1):
            loss_ref[i : i + 1, j * lanes : (j + 1) * lanes] = report_ref[2 * slot + j, :, lanes:]
    half = near_ref.shape[1]
    for h in (0, 1):
        cols = slice(h * half, (h + 1) * half)
        row_grad = jnp.where(place_ref[5] == h, near_ref[...], mate_ref[...])
        clipped = row_grad * clip_factor
        new_moment = beta_one * moment_ref[:, cols] + (1.0 - beta_one) * clipped
        new_second = beta_two * second_ref[:, cols] + (1.0 - beta_two) * clipped * clipped
        master = master_ref[:, cols]
        new_master_ref[:, cols] = master - learn_rate * (
            new_moment / (jnp.sqrt(new_second) + adam_eps) + weight_decay * master
        )
        new_moment_ref[:, cols] = new_moment
        new_second_ref[:, cols] = new_second


def front_kernel(
    group, y_rows, span_ref, place_ref, b_ref, own_ref, mate_ref, logit_ref, stat_ref, row_ref
):
    ctx, y_place, vocab_place = place_ref[0], place_ref[1], place_ref[2]
    tok = own_ref.shape[1]
    span = tok // 2
    quads = b_ref.shape[2] // NC
    small_ref = b_ref.at[:, :, :, b_ref.shape[3] - 2 * tok :]
    left, right = [], []
    for offset in (0, 1):
        sid = span_ref[2 * ctx + offset]
        at_z = (sid >> 2) & (NZ - 1)
        at_y = (y_place - (sid >> 5)) & (NY - 1)
        chip = small_ref[at_z, at_y].astype(f32)
        mine = jnp.where((sid & 2) == 0, chip[:quads], chip[quads:])
        odd = (sid & 1) == 1
        left.append(jnp.where(odd, mine[:, span:tok], mine[:, :span]))
        right.append(jnp.where(odd, mine[:, tok + span :], mine[:, tok : tok + span]))
    left = jnp.concatenate(left, 1)
    right = jnp.concatenate(right, 1)
    marks = jnp.sum(small_ref[:, :, :, :tok].astype(f32), axis=(0, 1))
    marks = marks[2:3] + marks[quads + 2 : quads + 3]
    token_count = jnp.sum(marks, axis=1, keepdims=True)
    target = left[0:1] * 256.0 + left[1:2]
    mask = left[2:3]
    local = target.astype(jnp.int32) - group * 4 - vocab_place * group
    ids = lax.broadcasted_iota(jnp.int32, (group, tok), 0)
    within = ids & (y_rows - 1)
    ids = ((y_place * y_rows - (ids - within)) & (group - 1)) + within
    hits = ids == local
    logits = own_ref[...] + mate_ref[...]
    logit_ref[...] = logits
    top = jnp.max(logits, axis=0, keepdims=True)
    stat_ref[0:1, :] = top
    stat_ref[1:2, :] = jnp.sum(jnp.exp(logits - top), axis=0, keepdims=True)
    stat_ref[2:3, :] = jnp.sum(jnp.where(hits, logits, 0.0), axis=0, keepdims=True)
    stat_ref[3:8, :] = jnp.zeros((5, tok), f32)
    row_ref[0:1, :] = target
    row_ref[1:2, :] = mask
    row_ref[2:3, :] = left[3:4] + right[0:1] + right[1:2]
    row_ref[3:4, :] = right[2:3] + right[3:4]
    row_ref[4:5, :] = mask * (loss_scale / token_count)
    row_ref[5:6, :] = jnp.broadcast_to(1.0 / token_count, (1, tok))
    row_ref[6:8, :] = jnp.zeros((2, tok), f32)


def square_kernel(a_ref, b0_ref, b1_ref, b2_ref, b3_ref, share_ref, grad_ref, report_ref):
    wide = a_ref.shape[2]
    part_a = a_ref[0].astype(f32)
    for i in range(1, a_ref.shape[0]):
        part_a = part_a + a_ref[i].astype(f32)
    part_b = b0_ref[...].astype(f32) + b1_ref[...].astype(f32)
    part_b = part_b + b2_ref[...].astype(f32) + b3_ref[...].astype(f32)
    grad_ref[:, :wide] = part_a
    grad_ref[:, wide:] = part_b
    total = jnp.sum(part_a * part_a, axis=1, keepdims=True)
    total = total + jnp.sum(part_b * part_b, axis=1, keepdims=True)
    total = jnp.sum(total, axis=0, keepdims=True)
    share = share_ref[...]
    row = jnp.concatenate([jnp.broadcast_to(total, share.shape), share], 1)
    report_ref[...] = jnp.broadcast_to(row[None], report_ref.shape)


VMEM = pl.BlockSpec(memory_space=pltpu.VMEM)
SMEM = pl.BlockSpec(memory_space=pltpu.SMEM)


def step(
    hidden_states, master, moment, second, targets, loss_mask, prior_lse, prior_target, span_order
):
    tok_rows, feat = hidden_states.shape
    shard_rows = master.shape[0]
    vocab_count = lax.axis_size("vocab")
    ctx_count = NY * NZ * NC
    core = lax.axis_index("core")
    y_place = lax.axis_index("y")
    vocab_place = lax.axis_index("vocab")
    ctx_place = (y_place * NZ + lax.axis_index("z")) * NC + core
    span = tok_rows // 2
    half = feat // 2
    group_rows = shard_rows * ctx_count
    block_total = group_rows * vocab_count
    y_rows = group_rows // NY
    chip_rows = y_rows // NZ

    thin = half // 16
    wide = half - thin
    thin_g = half * 3 // 16
    wide_g = half - thin_g
    halves = master.astype(bf16).reshape(shard_rows, NC, half)
    cut = halves[:, :, :wide].transpose(1, 0, 2)
    cut = jnp.broadcast_to(cut[None], (NZ,) + cut.shape).reshape(NZ * NC, shard_rows, wide)
    block = exchange(cut, ("z", "core")).reshape(y_rows, wide)
    digit = 256
    pieces = [targets // digit, targets % digit, loss_mask]
    pieces = [p.astype(f32) for p in pieces] + split(prior_lse, 3) + split(prior_target, 2)
    small = jnp.concatenate(
        [jnp.stack(pieces[:4], 0), jnp.stack(pieces[4:], 0)], 1
    ).astype(bf16)
    near_b = lax.dynamic_index_in_dim(halves[:, :, wide:], core, 1, keepdims=False)
    far_b = lax.dynamic_index_in_dim(halves[:, :, wide:], 1 - core, 1, keepdims=False)
    near_b = jnp.concatenate([near_b, small], 1)
    far_b = jnp.concatenate([far_b, small], 1)
    far_b = lax.ppermute(far_b, "core", SWAP)
    chip_b = pair(near_b, far_b, core == 0, 0)
    chips_b = jnp.stack([chip_b] + [shift(chip_b, "y", NY, s) for s in range(1, NY)], 0)
    parts_a = [block] + [shift(block, "y", NY, s) for s in range(1, NY)]
    part_b = spread(chips_b, "z", NZ)
    slot_ids = jnp.arange(span_order.shape[0], dtype=jnp.int32)
    slots = [
        jnp.sum(jnp.where(span_order == 2 * ctx_place + offset, slot_ids, 0))
        for offset in (0, 1)
    ]
    at = jnp.arange(8, dtype=jnp.int32)
    place = jnp.where(at == 0, ctx_place, jnp.where(at == 1, y_place, vocab_place))
    place = jnp.where(at == 3, slots[0], jnp.where(at == 4, slots[1], place))
    place = lax.optimization_barrier(jnp.where(at == 5, core, place))
    own_half = lax.dynamic_slice(
        hidden_states, (0, core * half), (tok_rows, half), allow_negative_indices=False
    )
    far_half = lax.dynamic_slice(
        hidden_states, (0, (1 - core) * half), (tok_rows, half), allow_negative_indices=False
    )
    mate_half = lax.ppermute(far_half, "core", SWAP)
    tokens = jnp.concatenate([own_half, mate_half], 0)

    def score(tok):
        return lax.dot_general(head, tok, (((1,), (1,)), ((), ())), preferred_element_type=f32)

    head, mate_part = pl.pallas_call(
        functools.partial(score_kernel, thin),
        out_shape=(
            jax.ShapeDtypeStruct((group_rows, half), bf16),
            jax.ShapeDtypeStruct((group_rows, tok_rows), f32),
        ),
        in_specs=[VMEM] * (NY + 2),
        out_specs=(VMEM, VMEM),
        name="score",
    )(*parts_a, part_b, mate_half)
    mate_head = lax.ppermute(head, "core", SWAP)
    mate_part = lax.ppermute(mate_part, "core", SWAP)
    own_part = score(own_half)
    logits, stats, rows = pl.pallas_call(
        functools.partial(front_kernel, group_rows, y_rows),
        out_shape=(
            jax.ShapeDtypeStruct((group_rows, tok_rows), f32),
            jax.ShapeDtypeStruct((8, tok_rows), f32),
            jax.ShapeDtypeStruct((8, tok_rows), f32),
        ),
        in_specs=[SMEM, SMEM, VMEM, VMEM, VMEM],
        out_specs=(VMEM, VMEM, VMEM),
        name="front",
    )(span_order, place, part_b, own_part, mate_part)
    tgt_rows = rows[0].astype(jnp.int32)
    mask_rows, prior_rows, outside, mask_scale = rows[1], rows[2], rows[3], rows[4]
    local_col = tgt_rows - block_total - vocab_place * group_rows
    vocab_ids = lax.broadcasted_iota(jnp.int32, (group_rows, tok_rows), 0)
    within = vocab_ids & (y_rows - 1)
    vocab_ids = ((y_place * y_rows - (vocab_ids - within)) & (group_rows - 1)) + within
    hits = vocab_ids == local_col[None, :]
    heard = [stats] + [shift(stats, "vocab", vocab_count, s) for s in range(1, vocab_count)]
    ordered = []
    for j in range(vocab_count):
        back = (vocab_place - j) % vocab_count
        pick = heard[0]
        for s in range(1, vocab_count):
            pick = jnp.where(back == s, heard[s], pick)
        ordered.append(pick)
    stats = jnp.stack(ordered, 0)
    top_value = jnp.maximum(prior_rows, jnp.max(stats[:, 0], axis=0))
    sum_total = jnp.sum(stats[:, 1] * jnp.exp(stats[:, 0] - top_value[None, :]), axis=0)
    target_sum = jnp.sum(stats[:, 2], axis=0)
    log_total = top_value + jnp.log(jnp.exp(prior_rows - top_value) + sum_total)
    target_logit = jnp.where(tgt_rows >= block_total, target_sum, outside)
    loss_rows = mask_rows * (log_total - target_logit)
    dlogits = (
        mask_scale[None, :] * (jnp.exp(logits - log_total[None, :]) - hits.astype(f32))
    ).astype(bf16)
    mate_dlogits = lax.ppermute(dlogits, "core", SWAP)

    both = jnp.concatenate([dlogits, mate_dlogits], 1)
    partial_rows = jnp.dot(both, tokens, preferred_element_type=f32).astype(bf16)
    blocks = [partial_rows[s * y_rows : (s + 1) * y_rows, :wide_g] for s in range(NY)]
    by_y = blocks[0].astype(f32)
    for s in range(1, NY):
        by_y = by_y + shift(blocks[s], "y", NY, -s).astype(f32)
    by_y = by_y.astype(bf16).reshape(NZ, chip_rows, wide_g)
    by_z = partial_rows[:, wide_g:].reshape(NY, NZ, chip_rows, thin_g).transpose(1, 0, 2, 3)
    by_z = jnp.sum(exchange(by_z, "z").astype(f32), axis=0).astype(bf16)
    pieces_b = [by_z[0]] + [shift(by_z[s], "y", NY, -s) for s in range(1, NY)]
    pieces_a = exchange(by_y, "z")
    lanes = tok_rows // vocab_count
    share = lax.dynamic_slice_in_dim(loss_rows, vocab_place * lanes, lanes, 0)
    share = share[None]
    chip_grad, report = pl.pallas_call(
        square_kernel,
        out_shape=(
            jax.ShapeDtypeStruct((chip_rows, half), f32),
            jax.ShapeDtypeStruct((ctx_count * vocab_count, 1, 2 * lanes), f32),
        ),
        in_specs=[VMEM] * (NY + 2),
        out_specs=(VMEM, VMEM),
        name="square",
    )(pieces_a, *pieces_b, share)
    reports = exchange(report, ALL)
    near = lax.dynamic_slice_in_dim(chip_grad, core * shard_rows, shard_rows, 0)
    far = lax.dynamic_slice_in_dim(chip_grad, (1 - core) * shard_rows, shard_rows, 0)
    mate = lax.ppermute(far, "core", SWAP)

    width = feat // vocab_count
    per_half = vocab_count // NC
    hidden_parts = []
    for s in range(vocab_count - 1, -1, -1):
        q = (vocab_place + s) & (vocab_count - 1)
        at = (q & (per_half - 1)) * width
        side = jnp.where(
            (q >= per_half) == (core == 1),
            lax.dynamic_slice(head, (0, at), (group_rows, width), allow_negative_indices=False),
            lax.dynamic_slice(
                mate_head, (0, at), (group_rows, width), allow_negative_indices=False
            ),
        )
        if s == 2:
            side = lax.optimization_barrier(side)
        part = lax.dot_general(
            dlogits, side, (((0,), (0,)), ((), ())), preferred_element_type=f32
        ).astype(bf16)
        if s:
            part = shift(part, "vocab", vocab_count, s)
        else:
            part = lax.optimization_barrier(part)
        hidden_parts.append(part)
    hidden_grad = sum(part.astype(f32) for part in hidden_parts).astype(bf16)

    state = jax.ShapeDtypeStruct((shard_rows, feat), f32)
    token_loss, mean_loss, new_master, new_moment, new_second = pl.pallas_call(
        final_kernel,
        out_shape=(
            jax.ShapeDtypeStruct((2, span), f32),
            jax.ShapeDtypeStruct((1, 1), f32),
            state,
            state,
            state,
        ),
        in_specs=[SMEM] + [VMEM] * 7,
        out_specs=(VMEM,) * 5,
        name="final",
    )(place, reports, rows, near, mate, master, moment, second)
    token_loss = token_loss.reshape(tok_rows)
    mean_loss = mean_loss[0, 0]
    return (token_loss, mean_loss, hidden_grad, new_master, new_moment, new_second)


def solution(mesh):
    grid = Mesh(mesh.devices.reshape(NY, NZ, NC, mesh.devices.shape[1]), ALL)
    head_spec = P(("vocab",) + CTX, None)
    in_specs = (
        P(CTX, None),
        head_spec,
        head_spec,
        head_spec,
        P(CTX),
        P(CTX),
        P(CTX),
        P(CTX),
        P(),
    )
    out_specs = (P(CTX), P(), P(CTX, "vocab"), head_spec, head_spec, head_spec)
    return jax.shard_map(step, mesh=grid, in_specs=in_specs, out_specs=out_specs, check_vma=False)
```

```python
import functools

import jax
import jax.numpy as jnp
from jax import lax
from jax.experimental import pallas as pl
from jax.experimental.pallas import tpu as pltpu
from jax.sharding import Mesh, PartitionSpec as P


loss_scale = 1048576.0
clip_norm = 0.004
beta_one = 0.9
beta_two = 0.95
learn_rate = 0.001
weight_decay = 0.1
adam_eps = 1e-08

NY, NZ, NC = 4, 8, 2
CTX = ("y", "z", "core")
ALL = ("y", "z", "core", "vocab")
SWAP = [(0, 1), (1, 0)]
f32 = jnp.float32
bf16 = jnp.bfloat16


def exchange(x, axes):
    return lax.all_to_all(x, axes, 0, 0, tiled=True)


def shift(x, axis, count, step):
    return lax.ppermute(x, axis, [(i, (i + step) % count) for i in range(count)])


def pair(x, y, keep, axis):
    return jnp.where(keep, jnp.concatenate([x, y], axis), jnp.concatenate([y, x], axis))


def split(x, count):
    out = []
    for _ in range(count):
        out.append(lax.reduce_precision(x, 8, 7))
        x = x - out[-1]
    return out


def spread(x, axes, count):
    return exchange(jnp.broadcast_to(x[None], (count,) + x.shape), axes)


def score_kernel(
    thin, a0_ref, a1_ref, a2_ref, a3_ref, b_ref, own_ref, mate_ref, head_ref, own_part_ref, mate_part_ref
):
    wide = a0_ref.shape[1]
    y_rows = a0_ref.shape[0]
    for s, a_ref in enumerate((a0_ref, a1_ref, a2_ref, a3_ref)):
        head_ref[s * y_rows : (s + 1) * y_rows, :wide] = a_ref[...]
        for z in range(NZ):
            at = s * y_rows + z * (y_rows // NZ)
            head_ref[at : at + y_rows // NZ, wide:] = b_ref[z, s, :, :thin]
    for tok_ref, part_ref in ((mate_ref, mate_part_ref), (own_ref, own_part_ref)):
        part_ref[...] = lax.dot_general(
            head_ref[...], tok_ref[...], (((1,), (1,)), ((), ())), preferred_element_type=f32
        )


def grad_kernel(own_d_ref, mate_d_ref, own_ref, mate_ref, a0_ref, a1_ref, a2_ref, a3_ref, b_ref):
    step = pl.program_id(0)
    cols = own_ref.shape[1]
    y_rows, wide = a0_ref.shape
    full, rest = wide // cols, wide % cols
    total = jnp.dot(own_d_ref[...], own_ref[...], preferred_element_type=f32)
    total = total + jnp.dot(mate_d_ref[...], mate_ref[...], preferred_element_type=f32)

    @pl.when(step < full)
    def _():
        at = pl.multiple_of(jnp.minimum(step, full - 1) * cols, cols)
        for s, a_ref in enumerate((a0_ref, a1_ref, a2_ref, a3_ref)):
            a_ref[:, pl.ds(at, cols)] = total[s * y_rows : (s + 1) * y_rows].astype(bf16)

    @pl.when(step == full)
    def _():
        for s, a_ref in enumerate((a0_ref, a1_ref, a2_ref, a3_ref)):
            a_ref[:, full * cols :] = total[s * y_rows : (s + 1) * y_rows, :rest].astype(bf16)
            for z in range(NZ):
                at = s * y_rows + z * (y_rows // NZ)
                b_ref[z, s] = total[at : at + y_rows // NZ, rest:].astype(bf16)


def final_kernel(
    place_ref, report_ref, row_ref, near_ref, mate_ref, master_ref, moment_ref, second_ref,
    loss_ref, mean_ref, new_master_ref, new_moment_ref, new_second_ref,
):
    sums = jnp.sum(report_ref[...], axis=0)
    norm_value = jnp.sqrt(sums[0:1, 0:1]) / loss_scale
    clip_factor = jnp.minimum(1.0, clip_norm / (norm_value + 1e-06))
    lanes = report_ref.shape[2] // 2
    mean_ref[...] = jnp.sum(sums[:, lanes:], axis=1, keepdims=True) * row_ref[5:6, 0:1]
    for i in (0, 1):
        slot = place_ref[3 + i]
        for j in (0, 1):
            loss_ref[i : i + 1, j * lanes : (j + 1) * lanes] = report_ref[2 * slot + j, :, lanes:]
    half = near_ref.shape[1]
    for h in (0, 1):
        cols = slice(h * half, (h + 1) * half)
        row_grad = jnp.where(place_ref[5] == h, near_ref[...], mate_ref[...])
        clipped = row_grad * clip_factor
        new_moment = beta_one * moment_ref[:, cols] + (1.0 - beta_one) * clipped
        new_second = beta_two * second_ref[:, cols] + (1.0 - beta_two) * clipped * clipped
        master = master_ref[:, cols]
        new_master_ref[:, cols] = master - learn_rate * (
            new_moment / (jnp.sqrt(new_second) + adam_eps) + weight_decay * master
        )
        new_moment_ref[:, cols] = new_moment
        new_second_ref[:, cols] = new_second


def front_kernel(
    group, y_rows, span_ref, place_ref, b_ref, own_ref, mate_ref, logit_ref, stat_ref, row_ref
):
    ctx, y_place, vocab_place = place_ref[0], place_ref[1], place_ref[2]
    tok = own_ref.shape[1]
    span = tok // 2
    quads = b_ref.shape[2] // NC
    small_ref = b_ref.at[:, :, :, b_ref.shape[3] - 2 * tok :]
    left, right = [], []
    for offset in (0, 1):
        sid = span_ref[2 * ctx + offset]
        at_z = (sid >> 2) & (NZ - 1)
        at_y = (y_place - (sid >> 5)) & (NY - 1)
        chip = small_ref[at_z, at_y].astype(f32)
        mine = jnp.where((sid & 2) == 0, chip[:quads], chip[quads:])
        odd = (sid & 1) == 1
        left.append(jnp.where(odd, mine[:, span:tok], mine[:, :span]))
        right.append(jnp.where(odd, mine[:, tok + span :], mine[:, tok : tok + span]))
    left = jnp.concatenate(left, 1)
    right = jnp.concatenate(right, 1)
    marks = jnp.sum(small_ref[:, :, :, :tok].astype(f32), axis=(0, 1))
    marks = marks[2:3] + marks[quads + 2 : quads + 3]
    token_count = jnp.sum(marks, axis=1, keepdims=True)
    target = left[0:1] * 256.0 + left[1:2]
    mask = left[2:3]
    local = target.astype(jnp.int32) - group * 4 - vocab_place * group
    ids = lax.broadcasted_iota(jnp.int32, (group, tok), 0)
    within = ids & (y_rows - 1)
    ids = ((y_place * y_rows - (ids - within)) & (group - 1)) + within
    hits = ids == local
    logits = own_ref[...] + mate_ref[...]
    logit_ref[...] = logits
    top = jnp.max(logits, axis=0, keepdims=True)
    stat_ref[0:1, :] = top
    stat_ref[1:2, :] = jnp.sum(jnp.exp(logits - top), axis=0, keepdims=True)
    stat_ref[2:3, :] = jnp.sum(jnp.where(hits, logits, 0.0), axis=0, keepdims=True)
    stat_ref[3:8, :] = jnp.zeros((5, tok), f32)
    row_ref[0:1, :] = target
    row_ref[1:2, :] = mask
    row_ref[2:3, :] = left[3:4] + right[0:1] + right[1:2]
    row_ref[3:4, :] = right[2:3] + right[3:4]
    row_ref[4:5, :] = mask * (loss_scale / token_count)
    row_ref[5:6, :] = jnp.broadcast_to(1.0 / token_count, (1, tok))
    row_ref[6:8, :] = jnp.zeros((2, tok), f32)


def square_kernel(a_ref, b0_ref, b1_ref, b2_ref, b3_ref, share_ref, grad_ref, report_ref):
    wide = a_ref.shape[2]
    part_a = a_ref[0].astype(f32)
    for i in range(1, a_ref.shape[0]):
        part_a = part_a + a_ref[i].astype(f32)
    part_b = b0_ref[...].astype(f32) + b1_ref[...].astype(f32)
    part_b = part_b + b2_ref[...].astype(f32) + b3_ref[...].astype(f32)
    grad_ref[:, :wide] = part_a
    grad_ref[:, wide:] = part_b
    total = jnp.sum(part_a * part_a, axis=1, keepdims=True)
    total = total + jnp.sum(part_b * part_b, axis=1, keepdims=True)
    total = jnp.sum(total, axis=0, keepdims=True)
    share = share_ref[...]
    row = jnp.concatenate([jnp.broadcast_to(total, share.shape), share], 1)
    report_ref[...] = jnp.broadcast_to(row[None], report_ref.shape)


VMEM = pl.BlockSpec(memory_space=pltpu.VMEM)
SMEM = pl.BlockSpec(memory_space=pltpu.SMEM)


def step(
    hidden_states, master, moment, second, targets, loss_mask, prior_lse, prior_target, span_order
):
    tok_rows, feat = hidden_states.shape
    shard_rows = master.shape[0]
    vocab_count = lax.axis_size("vocab")
    ctx_count = NY * NZ * NC
    core = lax.axis_index("core")
    y_place = lax.axis_index("y")
    vocab_place = lax.axis_index("vocab")
    ctx_place = (y_place * NZ + lax.axis_index("z")) * NC + core
    span = tok_rows // 2
    half = feat // 2
    group_rows = shard_rows * ctx_count
    block_total = group_rows * vocab_count
    y_rows = group_rows // NY
    chip_rows = y_rows // NZ

    thin = half // 16
    wide = half - thin
    thin_g = half * 3 // 16
    wide_g = half - thin_g
    halves = master.astype(bf16).reshape(shard_rows, NC, half)
    cut = halves[:, :, :wide].transpose(1, 0, 2)
    cut = jnp.broadcast_to(cut[None], (NZ,) + cut.shape).reshape(NZ * NC, shard_rows, wide)
    block = exchange(cut, ("z", "core")).reshape(y_rows, wide)
    digit = 256
    pieces = [targets // digit, targets % digit, loss_mask]
    pieces = [p.astype(f32) for p in pieces] + split(prior_lse, 3) + split(prior_target, 2)
    small = jnp.concatenate(
        [jnp.stack(pieces[:4], 0), jnp.stack(pieces[4:], 0)], 1
    ).astype(bf16)
    near_b = lax.dynamic_index_in_dim(halves[:, :, wide:], core, 1, keepdims=False)
    far_b = lax.dynamic_index_in_dim(halves[:, :, wide:], 1 - core, 1, keepdims=False)
    near_b = jnp.concatenate([near_b, small], 1)
    far_b = jnp.concatenate([far_b, small], 1)
    far_b = lax.ppermute(far_b, "core", SWAP)
    chip_b = pair(near_b, far_b, core == 0, 0)
    chips_b = jnp.stack([chip_b] + [shift(chip_b, "y", NY, s) for s in range(1, NY)], 0)
    parts_a = [block] + [shift(block, "y", NY, s) for s in range(1, NY)]
    part_b = spread(chips_b, "z", NZ)
    slot_ids = jnp.arange(span_order.shape[0], dtype=jnp.int32)
    slots = [
        jnp.sum(jnp.where(span_order == 2 * ctx_place + offset, slot_ids, 0))
        for offset in (0, 1)
    ]
    at = jnp.arange(8, dtype=jnp.int32)
    place = jnp.where(at == 0, ctx_place, jnp.where(at == 1, y_place, vocab_place))
    place = jnp.where(at == 3, slots[0], jnp.where(at == 4, slots[1], place))
    place = lax.optimization_barrier(jnp.where(at == 5, core, place))
    own_half = lax.dynamic_slice(
        hidden_states, (0, core * half), (tok_rows, half), allow_negative_indices=False
    )
    far_half = lax.dynamic_slice(
        hidden_states, (0, (1 - core) * half), (tok_rows, half), allow_negative_indices=False
    )
    mate_half = lax.ppermute(far_half, "core", SWAP)

    head, own_part, mate_part = pl.pallas_call(
        functools.partial(score_kernel, thin),
        out_shape=(
            jax.ShapeDtypeStruct((group_rows, half), bf16),
            jax.ShapeDtypeStruct((group_rows, tok_rows), f32),
            jax.ShapeDtypeStruct((group_rows, tok_rows), f32),
        ),
        in_specs=[VMEM] * (NY + 3),
        out_specs=(VMEM, VMEM, VMEM),
        name="score",
    )(*parts_a, part_b, own_half, mate_half)
    mate_head = lax.ppermute(head, "core", SWAP)
    mate_part = lax.ppermute(mate_part, "core", SWAP)
    logits, stats, rows = pl.pallas_call(
        functools.partial(front_kernel, group_rows, y_rows),
        out_shape=(
            jax.ShapeDtypeStruct((group_rows, tok_rows), f32),
            jax.ShapeDtypeStruct((8, tok_rows), f32),
            jax.ShapeDtypeStruct((8, tok_rows), f32),
        ),
        in_specs=[SMEM, SMEM, VMEM, VMEM, VMEM],
        out_specs=(VMEM, VMEM, VMEM),
        name="front",
    )(span_order, place, part_b, own_part, mate_part)
    tgt_rows = rows[0].astype(jnp.int32)
    mask_rows, prior_rows, outside, mask_scale = rows[1], rows[2], rows[3], rows[4]
    local_col = tgt_rows - block_total - vocab_place * group_rows
    vocab_ids = lax.broadcasted_iota(jnp.int32, (group_rows, tok_rows), 0)
    within = vocab_ids & (y_rows - 1)
    vocab_ids = ((y_place * y_rows - (vocab_ids - within)) & (group_rows - 1)) + within
    hits = vocab_ids == local_col[None, :]
    heard = [stats] + [shift(stats, "vocab", vocab_count, s) for s in range(1, vocab_count)]
    ordered = []
    for j in range(vocab_count):
        back = (vocab_place - j) % vocab_count
        pick = heard[0]
        for s in range(1, vocab_count):
            pick = jnp.where(back == s, heard[s], pick)
        ordered.append(pick)
    stats = jnp.stack(ordered, 0)
    top_value = jnp.maximum(prior_rows, jnp.max(stats[:, 0], axis=0))
    sum_total = jnp.sum(stats[:, 1] * jnp.exp(stats[:, 0] - top_value[None, :]), axis=0)
    target_sum = jnp.sum(stats[:, 2], axis=0)
    log_total = top_value + jnp.log(jnp.exp(prior_rows - top_value) + sum_total)
    target_logit = jnp.where(tgt_rows >= block_total, target_sum, outside)
    loss_rows = mask_rows * (log_total - target_logit)
    dlogits = (
        mask_scale[None, :] * (jnp.exp(logits - log_total[None, :]) - hits.astype(f32))
    ).astype(bf16)
    mate_dlogits = lax.ppermute(dlogits, "core", SWAP)

    cols = half // 4
    block_shape = jax.ShapeDtypeStruct((y_rows, wide_g), bf16)
    fixed = pl.BlockSpec((y_rows, wide_g), lambda i: (0, 0))
    dlog_spec = pl.BlockSpec((group_rows, tok_rows), lambda i: (0, 0))
    tok_spec = pl.BlockSpec((tok_rows, cols), lambda i: (0, i))
    *blocks, by_z = pl.pallas_call(
        grad_kernel,
        grid=(half // cols,),
        out_shape=[block_shape] * NY
        + [jax.ShapeDtypeStruct((NZ, NY, chip_rows, thin_g), bf16)],
        in_specs=[dlog_spec, dlog_spec, tok_spec, tok_spec],
        out_specs=[fixed] * NY
        + [pl.BlockSpec((NZ, NY, chip_rows, thin_g), lambda i: (0, 0, 0, 0))],
        name="grad",
    )(dlogits, mate_dlogits, own_half, mate_half)
    by_y = blocks[0].astype(f32)
    for s in range(1, NY):
        by_y = by_y + shift(blocks[s], "y", NY, -s).astype(f32)
    by_y = by_y.astype(bf16).reshape(NZ, chip_rows, wide_g)
    by_z = jnp.sum(exchange(by_z, "z").astype(f32), axis=0).astype(bf16)
    pieces_b = [by_z[0]] + [shift(by_z[s], "y", NY, -s) for s in range(1, NY)]
    pieces_a = exchange(by_y, "z")
    lanes = tok_rows // vocab_count
    share = lax.dynamic_slice_in_dim(loss_rows, vocab_place * lanes, lanes, 0)
    share = share[None]
    chip_grad, report = pl.pallas_call(
        square_kernel,
        out_shape=(
            jax.ShapeDtypeStruct((chip_rows, half), f32),
            jax.ShapeDtypeStruct((ctx_count * vocab_count, 1, 2 * lanes), f32),
        ),
        in_specs=[VMEM] * (NY + 2),
        out_specs=(VMEM, VMEM),
        name="square",
    )(pieces_a, *pieces_b, share)
    reports = exchange(report, ALL)
    near = lax.dynamic_slice_in_dim(chip_grad, core * shard_rows, shard_rows, 0)
    far = lax.dynamic_slice_in_dim(chip_grad, (1 - core) * shard_rows, shard_rows, 0)
    mate = lax.ppermute(far, "core", SWAP)

    width = feat // vocab_count
    per_half = vocab_count // NC
    hidden_parts = []
    for s in range(vocab_count - 1, -1, -1):
        q = (vocab_place + s) & (vocab_count - 1)
        at = (q & (per_half - 1)) * width
        side = jnp.where(
            (q >= per_half) == (core == 1),
            lax.dynamic_slice(head, (0, at), (group_rows, width), allow_negative_indices=False),
            lax.dynamic_slice(
                mate_head, (0, at), (group_rows, width), allow_negative_indices=False
            ),
        )
        if s == 2:
            side = lax.optimization_barrier(side)
        part = lax.dot_general(
            dlogits, side, (((0,), (0,)), ((), ())), preferred_element_type=f32
        ).astype(bf16)
        if s:
            part = shift(part, "vocab", vocab_count, s)
        else:
            part = lax.optimization_barrier(part)
        hidden_parts.append(part)
    hidden_grad = sum(part.astype(f32) for part in hidden_parts).astype(bf16)

    state = jax.ShapeDtypeStruct((shard_rows, feat), f32)
    token_loss, mean_loss, new_master, new_moment, new_second = pl.pallas_call(
        final_kernel,
        out_shape=(
            jax.ShapeDtypeStruct((2, span), f32),
            jax.ShapeDtypeStruct((1, 1), f32),
            state,
            state,
            state,
        ),
        in_specs=[SMEM] + [VMEM] * 7,
        out_specs=(VMEM,) * 5,
        name="final",
    )(place, reports, rows, near, mate, master, moment, second)
    token_loss = token_loss.reshape(tok_rows)
    mean_loss = mean_loss[0, 0]
    return (token_loss, mean_loss, hidden_grad, new_master, new_moment, new_second)


def solution(mesh):
    grid = Mesh(mesh.devices.reshape(NY, NZ, NC, mesh.devices.shape[1]), ALL)
    head_spec = P(("vocab",) + CTX, None)
    in_specs = (
        P(CTX, None),
        head_spec,
        head_spec,
        head_spec,
        P(CTX),
        P(CTX),
        P(CTX),
        P(CTX),
        P(),
    )
    out_specs = (P(CTX), P(), P(CTX, "vocab"), head_spec, head_spec, head_spec)
    return jax.shard_map(step, mesh=grid, in_specs=in_specs, out_specs=out_specs, check_vma=False)
```

```python
import functools

import jax
import jax.numpy as jnp
from jax import lax
from jax.experimental import pallas as pl
from jax.experimental.pallas import tpu as pltpu
from jax.sharding import Mesh, PartitionSpec as P


loss_scale = 1048576.0
clip_norm = 0.004
beta_one = 0.9
beta_two = 0.95
learn_rate = 0.001
weight_decay = 0.1
adam_eps = 1e-08

NY, NZ, NC = 4, 8, 2
CTX = ("y", "z", "core")
ALL = ("y", "z", "core", "vocab")
SWAP = [(0, 1), (1, 0)]
f32 = jnp.float32
bf16 = jnp.bfloat16


def exchange(x, axes):
    return lax.all_to_all(x, axes, 0, 0, tiled=True)


def shift(x, axis, count, step):
    return lax.ppermute(x, axis, [(i, (i + step) % count) for i in range(count)])


def pair(x, y, keep, axis):
    return jnp.where(keep, jnp.concatenate([x, y], axis), jnp.concatenate([y, x], axis))


def split(x, count):
    out = []
    for _ in range(count):
        out.append(lax.reduce_precision(x, 8, 7))
        x = x - out[-1]
    return out


def spread(x, axes, count):
    return exchange(jnp.broadcast_to(x[None], (count,) + x.shape), axes)


def score_kernel(
    a0_ref, a1_ref, a2_ref, a3_ref, b_ref, own_ref, mate_ref, head_ref, own_part_ref, mate_part_ref
):
    step = pl.program_id(0)
    last = pl.num_programs(0) - 1
    y_rows, cols = a0_ref.shape

    @pl.when(step < last)
    def _():
        for s, a_ref in enumerate((a0_ref, a1_ref, a2_ref, a3_ref)):
            head_ref[s * y_rows : (s + 1) * y_rows, :] = a_ref[...]

    @pl.when(step == last)
    def _():
        for s in range(NY):
            for z in range(NZ):
                at = s * y_rows + z * (y_rows // NZ)
                head_ref[at : at + y_rows // NZ, :] = b_ref[z, s, :, :cols]

    @pl.when(step == 0)
    def _():
        own_part_ref[...] = jnp.zeros(own_part_ref.shape, f32)
        mate_part_ref[...] = jnp.zeros(mate_part_ref.shape, f32)

    for tok_ref, part_ref in ((mate_ref, mate_part_ref), (own_ref, own_part_ref)):
        part_ref[...] += lax.dot_general(
            head_ref[...], tok_ref[...], (((1,), (1,)), ((), ())), preferred_element_type=f32
        )


def final_kernel(
    place_ref, report_ref, row_ref, near_ref, mate_ref, master_ref, moment_ref, second_ref,
    loss_ref, mean_ref, new_master_ref, new_moment_ref, new_second_ref,
):
    sums = jnp.sum(report_ref[...], axis=0)
    norm_value = jnp.sqrt(sums[0:1, 0:1]) / loss_scale
    clip_factor = jnp.minimum(1.0, clip_norm / (norm_value + 1e-06))
    lanes = report_ref.shape[2] // 2
    mean_ref[...] = jnp.sum(sums[:, lanes:], axis=1, keepdims=True) * row_ref[5:6, 0:1]
    for i in (0, 1):
        slot = place_ref[3 + i]
        for j in (0, 1):
            loss_ref[i : i + 1, j * lanes : (j + 1) * lanes] = report_ref[2 * slot + j, :, lanes:]
    half = near_ref.shape[1]
    for h in (0, 1):
        cols = slice(h * half, (h + 1) * half)
        row_grad = jnp.where(place_ref[5] == h, near_ref[...], mate_ref[...])
        clipped = row_grad * clip_factor
        new_moment = beta_one * moment_ref[:, cols] + (1.0 - beta_one) * clipped
        new_second = beta_two * second_ref[:, cols] + (1.0 - beta_two) * clipped * clipped
        master = master_ref[:, cols]
        new_master_ref[:, cols] = master - learn_rate * (
            new_moment / (jnp.sqrt(new_second) + adam_eps) + weight_decay * master
        )
        new_moment_ref[:, cols] = new_moment
        new_second_ref[:, cols] = new_second


def front_kernel(
    group, y_rows, span_ref, place_ref, b_ref, own_ref, mate_ref, logit_ref, stat_ref, row_ref
):
    ctx, y_place, vocab_place = place_ref[0], place_ref[1], place_ref[2]
    tok = own_ref.shape[1]
    span = tok // 2
    quads = b_ref.shape[2] // NC
    small_ref = b_ref.at[:, :, :, b_ref.shape[3] - 2 * tok :]
    left, right = [], []
    for offset in (0, 1):
        sid = span_ref[2 * ctx + offset]
        at_z = (sid >> 2) & (NZ - 1)
        at_y = (y_place - (sid >> 5)) & (NY - 1)
        chip = small_ref[at_z, at_y].astype(f32)
        mine = jnp.where((sid & 2) == 0, chip[:quads], chip[quads:])
        odd = (sid & 1) == 1
        left.append(jnp.where(odd, mine[:, span:tok], mine[:, :span]))
        right.append(jnp.where(odd, mine[:, tok + span :], mine[:, tok : tok + span]))
    left = jnp.concatenate(left, 1)
    right = jnp.concatenate(right, 1)
    marks = jnp.sum(small_ref[:, :, :, :tok].astype(f32), axis=(0, 1))
    marks = marks[2:3] + marks[quads + 2 : quads + 3]
    token_count = jnp.sum(marks, axis=1, keepdims=True)
    target = left[0:1] * 256.0 + left[1:2]
    mask = left[2:3]
    local = target.astype(jnp.int32) - group * 4 - vocab_place * group
    ids = lax.broadcasted_iota(jnp.int32, (group, tok), 0)
    within = ids & (y_rows - 1)
    ids = ((y_place * y_rows - (ids - within)) & (group - 1)) + within
    hits = ids == local
    logits = own_ref[...] + mate_ref[...]
    logit_ref[...] = logits
    top = jnp.max(logits, axis=0, keepdims=True)
    stat_ref[0:1, :] = top
    stat_ref[1:2, :] = jnp.sum(jnp.exp(logits - top), axis=0, keepdims=True)
    stat_ref[2:3, :] = jnp.sum(jnp.where(hits, logits, 0.0), axis=0, keepdims=True)
    stat_ref[3:8, :] = jnp.zeros((5, tok), f32)
    row_ref[0:1, :] = target
    row_ref[1:2, :] = mask
    row_ref[2:3, :] = left[3:4] + right[0:1] + right[1:2]
    row_ref[3:4, :] = right[2:3] + right[3:4]
    row_ref[4:5, :] = mask * (loss_scale / token_count)
    row_ref[5:6, :] = jnp.broadcast_to(1.0 / token_count, (1, tok))
    row_ref[6:8, :] = jnp.zeros((2, tok), f32)


def square_kernel(a_ref, b0_ref, b1_ref, b2_ref, b3_ref, share_ref, grad_ref, report_ref):
    wide = a_ref.shape[2]
    part_a = a_ref[0].astype(f32)
    for i in range(1, a_ref.shape[0]):
        part_a = part_a + a_ref[i].astype(f32)
    part_b = b0_ref[...].astype(f32) + b1_ref[...].astype(f32)
    part_b = part_b + b2_ref[...].astype(f32) + b3_ref[...].astype(f32)
    grad_ref[:, :wide] = part_a
    grad_ref[:, wide:] = part_b
    total = jnp.sum(part_a * part_a, axis=1, keepdims=True)
    total = total + jnp.sum(part_b * part_b, axis=1, keepdims=True)
    total = jnp.sum(total, axis=0, keepdims=True)
    share = share_ref[...]
    row = jnp.concatenate([jnp.broadcast_to(total, share.shape), share], 1)
    report_ref[...] = jnp.broadcast_to(row[None], report_ref.shape)


VMEM = pl.BlockSpec(memory_space=pltpu.VMEM)
SMEM = pl.BlockSpec(memory_space=pltpu.SMEM)


def step(
    hidden_states, master, moment, second, targets, loss_mask, prior_lse, prior_target, span_order
):
    tok_rows, feat = hidden_states.shape
    shard_rows = master.shape[0]
    vocab_count = lax.axis_size("vocab")
    ctx_count = NY * NZ * NC
    core = lax.axis_index("core")
    y_place = lax.axis_index("y")
    vocab_place = lax.axis_index("vocab")
    ctx_place = (y_place * NZ + lax.axis_index("z")) * NC + core
    span = tok_rows // 2
    half = feat // 2
    group_rows = shard_rows * ctx_count
    block_total = group_rows * vocab_count
    y_rows = group_rows // NY
    chip_rows = y_rows // NZ

    thin = half // 8
    wide = half - thin
    thin_g = half * 3 // 16
    wide_g = half - thin_g
    halves = master.astype(bf16).reshape(shard_rows, NC, half)
    cut = halves[:, :, :wide].transpose(1, 0, 2)
    cut = jnp.broadcast_to(cut[None], (NZ,) + cut.shape).reshape(NZ * NC, shard_rows, wide)
    block = exchange(cut, ("z", "core")).reshape(y_rows, wide)
    digit = 256
    pieces = [targets // digit, targets % digit, loss_mask]
    pieces = [p.astype(f32) for p in pieces] + split(prior_lse, 3) + split(prior_target, 2)
    small = jnp.concatenate(
        [jnp.stack(pieces[:4], 0), jnp.stack(pieces[4:], 0)], 1
    ).astype(bf16)
    near_b = lax.dynamic_index_in_dim(halves[:, :, wide:], core, 1, keepdims=False)
    far_b = lax.dynamic_index_in_dim(halves[:, :, wide:], 1 - core, 1, keepdims=False)
    near_b = jnp.concatenate([near_b, small], 1)
    far_b = jnp.concatenate([far_b, small], 1)
    far_b = lax.ppermute(far_b, "core", SWAP)
    chip_b = pair(near_b, far_b, core == 0, 0)
    chips_b = jnp.stack([chip_b] + [shift(chip_b, "y", NY, s) for s in range(1, NY)], 0)
    parts_a = [block] + [shift(block, "y", NY, s) for s in range(1, NY)]
    part_b = spread(chips_b, "z", NZ)
    slot_ids = jnp.arange(span_order.shape[0], dtype=jnp.int32)
    slots = [
        jnp.sum(jnp.where(span_order == 2 * ctx_place + offset, slot_ids, 0))
        for offset in (0, 1)
    ]
    at = jnp.arange(8, dtype=jnp.int32)
    place = jnp.where(at == 0, ctx_place, jnp.where(at == 1, y_place, vocab_place))
    place = jnp.where(at == 3, slots[0], jnp.where(at == 4, slots[1], place))
    place = lax.optimization_barrier(jnp.where(at == 5, core, place))
    own_half = lax.dynamic_slice(
        hidden_states, (0, core * half), (tok_rows, half), allow_negative_indices=False
    )
    far_half = lax.dynamic_slice(
        hidden_states, (0, (1 - core) * half), (tok_rows, half), allow_negative_indices=False
    )
    mate_half = lax.ppermute(far_half, "core", SWAP)
    tokens = jnp.concatenate([own_half, mate_half], 0)

    steps = half // thin
    block_a = pl.BlockSpec((y_rows, thin), lambda i: (0, jnp.minimum(i, steps - 2)))
    block_t = pl.BlockSpec((tok_rows, thin), lambda i: (0, i))
    block_p = pl.BlockSpec((group_rows, tok_rows), lambda i: (0, 0))
    head, own_part, mate_part = pl.pallas_call(
        score_kernel,
        grid=(steps,),
        out_shape=(
            jax.ShapeDtypeStruct((group_rows, half), bf16),
            jax.ShapeDtypeStruct((group_rows, tok_rows), f32),
            jax.ShapeDtypeStruct((group_rows, tok_rows), f32),
        ),
        in_specs=[block_a] * NY
        + [pl.BlockSpec(part_b.shape, lambda i: (0, 0, 0, 0)), block_t, block_t],
        out_specs=(pl.BlockSpec((group_rows, thin), lambda i: (0, i)), block_p, block_p),
        name="score",
    )(*parts_a, part_b, own_half, mate_half)
    mate_part = lax.ppermute(mate_part, "core", SWAP)
    mate_head = lax.ppermute(head, "core", SWAP)
    logits, stats, rows = pl.pallas_call(
        functools.partial(front_kernel, group_rows, y_rows),
        out_shape=(
            jax.ShapeDtypeStruct((group_rows, tok_rows), f32),
            jax.ShapeDtypeStruct((8, tok_rows), f32),
            jax.ShapeDtypeStruct((8, tok_rows), f32),
        ),
        in_specs=[SMEM, SMEM, VMEM, VMEM, VMEM],
        out_specs=(VMEM, VMEM, VMEM),
        name="front",
    )(span_order, place, part_b, own_part, mate_part)
    tgt_rows = rows[0].astype(jnp.int32)
    mask_rows, prior_rows, outside, mask_scale = rows[1], rows[2], rows[3], rows[4]
    local_col = tgt_rows - block_total - vocab_place * group_rows
    vocab_ids = lax.broadcasted_iota(jnp.int32, (group_rows, tok_rows), 0)
    within = vocab_ids & (y_rows - 1)
    vocab_ids = ((y_place * y_rows - (vocab_ids - within)) & (group_rows - 1)) + within
    hits = vocab_ids == local_col[None, :]
    heard = [stats] + [shift(stats, "vocab", vocab_count, s) for s in range(1, vocab_count)]
    ordered = []
    for j in range(vocab_count):
        back = (vocab_place - j) % vocab_count
        pick = heard[0]
        for s in range(1, vocab_count):
            pick = jnp.where(back == s, heard[s], pick)
        ordered.append(pick)
    stats = jnp.stack(ordered, 0)
    top_value = jnp.maximum(prior_rows, jnp.max(stats[:, 0], axis=0))
    sum_total = jnp.sum(stats[:, 1] * jnp.exp(stats[:, 0] - top_value[None, :]), axis=0)
    target_sum = jnp.sum(stats[:, 2], axis=0)
    log_total = top_value + jnp.log(jnp.exp(prior_rows - top_value) + sum_total)
    target_logit = jnp.where(tgt_rows >= block_total, target_sum, outside)
    loss_rows = mask_rows * (log_total - target_logit)
    dlogits = (
        mask_scale[None, :] * (jnp.exp(logits - log_total[None, :]) - hits.astype(f32))
    ).astype(bf16)
    mate_dlogits = lax.ppermute(dlogits, "core", SWAP)

    both = jnp.concatenate([dlogits, mate_dlogits], 1)
    partial_rows = jnp.dot(both, tokens, preferred_element_type=f32).astype(bf16)
    blocks = [partial_rows[s * y_rows : (s + 1) * y_rows, :wide_g] for s in range(NY)]
    by_y = blocks[0].astype(f32)
    for s in range(1, NY):
        by_y = by_y + shift(blocks[s], "y", NY, -s).astype(f32)
    by_y = by_y.astype(bf16).reshape(NZ, chip_rows, wide_g)
    by_z = partial_rows[:, wide_g:].reshape(NY, NZ, chip_rows, thin_g).transpose(1, 0, 2, 3)
    by_z = jnp.sum(exchange(by_z, "z").astype(f32), axis=0).astype(bf16)
    pieces_b = [by_z[0]] + [shift(by_z[s], "y", NY, -s) for s in range(1, NY)]
    pieces_a = exchange(by_y, "z")
    lanes = tok_rows // vocab_count
    share = lax.dynamic_slice_in_dim(loss_rows, vocab_place * lanes, lanes, 0)
    share = share[None]
    chip_grad, report = pl.pallas_call(
        square_kernel,
        out_shape=(
            jax.ShapeDtypeStruct((chip_rows, half), f32),
            jax.ShapeDtypeStruct((ctx_count * vocab_count, 1, 2 * lanes), f32),
        ),
        in_specs=[VMEM] * (NY + 2),
        out_specs=(VMEM, VMEM),
        name="square",
    )(pieces_a, *pieces_b, share)
    reports = exchange(report, ALL)
    near = lax.dynamic_slice_in_dim(chip_grad, core * shard_rows, shard_rows, 0)
    far = lax.dynamic_slice_in_dim(chip_grad, (1 - core) * shard_rows, shard_rows, 0)
    mate = lax.ppermute(far, "core", SWAP)

    width = feat // vocab_count
    per_half = vocab_count // NC
    hidden_parts = []
    for s in range(vocab_count - 1, -1, -1):
        q = (vocab_place + s) & (vocab_count - 1)
        at = (q & (per_half - 1)) * width
        side = jnp.where(
            (q >= per_half) == (core == 1),
            lax.dynamic_slice(head, (0, at), (group_rows, width), allow_negative_indices=False),
            lax.dynamic_slice(
                mate_head, (0, at), (group_rows, width), allow_negative_indices=False
            ),
        )
        if s == 2:
            side = lax.optimization_barrier(side)
        part = lax.dot_general(
            dlogits, side, (((0,), (0,)), ((), ())), preferred_element_type=f32
        ).astype(bf16)
        if s:
            part = shift(part, "vocab", vocab_count, s)
        else:
            part = lax.optimization_barrier(part)
        hidden_parts.append(part)
    hidden_grad = sum(part.astype(f32) for part in hidden_parts).astype(bf16)

    state = jax.ShapeDtypeStruct((shard_rows, feat), f32)
    token_loss, mean_loss, new_master, new_moment, new_second = pl.pallas_call(
        final_kernel,
        out_shape=(
            jax.ShapeDtypeStruct((2, span), f32),
            jax.ShapeDtypeStruct((1, 1), f32),
            state,
            state,
            state,
        ),
        in_specs=[SMEM] + [VMEM] * 7,
        out_specs=(VMEM,) * 5,
        name="final",
    )(place, reports, rows, near, mate, master, moment, second)
    token_loss = token_loss.reshape(tok_rows)
    mean_loss = mean_loss[0, 0]
    return (token_loss, mean_loss, hidden_grad, new_master, new_moment, new_second)


def solution(mesh):
    grid = Mesh(mesh.devices.reshape(NY, NZ, NC, mesh.devices.shape[1]), ALL)
    head_spec = P(("vocab",) + CTX, None)
    in_specs = (
        P(CTX, None),
        head_spec,
        head_spec,
        head_spec,
        P(CTX),
        P(CTX),
        P(CTX),
        P(CTX),
        P(),
    )
    out_specs = (P(CTX), P(), P(CTX, "vocab"), head_spec, head_spec, head_spec)
    return jax.shard_map(step, mesh=grid, in_specs=in_specs, out_specs=out_specs, check_vma=False)
```

```python
import functools

import jax
import jax.numpy as jnp
from jax import lax
from jax.experimental import pallas as pl
from jax.experimental.pallas import tpu as pltpu
from jax.sharding import Mesh, PartitionSpec as P


loss_scale = 1048576.0
clip_norm = 0.004
beta_one = 0.9
beta_two = 0.95
learn_rate = 0.001
weight_decay = 0.1
adam_eps = 1e-08

NY, NZ, NC = 4, 8, 2
CTX = ("y", "z", "core")
ALL = ("y", "z", "core", "vocab")
SWAP = [(0, 1), (1, 0)]
f32 = jnp.float32
bf16 = jnp.bfloat16


def exchange(x, axes):
    return lax.all_to_all(x, axes, 0, 0, tiled=True)


def shift(x, axis, count, step):
    return lax.ppermute(x, axis, [(i, (i + step) % count) for i in range(count)])


def pair(x, y, keep, axis):
    return jnp.where(keep, jnp.concatenate([x, y], axis), jnp.concatenate([y, x], axis))


def split(x, count):
    out = []
    for _ in range(count):
        out.append(lax.reduce_precision(x, 8, 7))
        x = x - out[-1]
    return out


def spread(x, axes, count):
    return exchange(jnp.broadcast_to(x[None], (count,) + x.shape), axes)


def score_kernel(
    thin, a0_ref, a1_ref, a2_ref, a3_ref, b_ref, own_ref, mate_ref, head_ref, own_part_ref, mate_part_ref
):
    wide = a0_ref.shape[1]
    y_rows = a0_ref.shape[0]
    for s, a_ref in enumerate((a0_ref, a1_ref, a2_ref, a3_ref)):
        head_ref[s * y_rows : (s + 1) * y_rows, :wide] = a_ref[...]
        for z in range(NZ):
            at = s * y_rows + z * (y_rows // NZ)
            head_ref[at : at + y_rows // NZ, wide:] = b_ref[z, s, :, :thin]
    for tok_ref, part_ref in ((mate_ref, mate_part_ref), (own_ref, own_part_ref)):
        part_ref[...] = lax.dot_general(
            head_ref[...], tok_ref[...], (((1,), (1,)), ((), ())), preferred_element_type=f32
        )


def final_kernel(
    place_ref, report_ref, row_ref, near_ref, mate_ref, master_ref, moment_ref, second_ref,
    loss_ref, mean_ref, new_master_ref, new_moment_ref, new_second_ref,
):
    sums = jnp.sum(report_ref[...], axis=0)
    norm_value = jnp.sqrt(sums[0:1, 0:1]) / loss_scale
    clip_factor = jnp.minimum(1.0, clip_norm / (norm_value + 1e-06))
    lanes = report_ref.shape[2] // 2
    mean_ref[...] = jnp.sum(sums[:, lanes:], axis=1, keepdims=True) * row_ref[5:6, 0:1]
    for i in (0, 1):
        slot = place_ref[3 + i]
        for j in (0, 1):
            loss_ref[i : i + 1, j * lanes : (j + 1) * lanes] = report_ref[2 * slot + j, :, lanes:]
    half = near_ref.shape[1]
    for h in (0, 1):
        cols = slice(h * half, (h + 1) * half)
        row_grad = jnp.where(place_ref[5] == h, near_ref[...], mate_ref[...])
        clipped = row_grad * clip_factor
        new_moment = beta_one * moment_ref[:, cols] + (1.0 - beta_one) * clipped
        new_second = beta_two * second_ref[:, cols] + (1.0 - beta_two) * clipped * clipped
        master = master_ref[:, cols]
        new_master_ref[:, cols] = master - learn_rate * (
            new_moment / (jnp.sqrt(new_second) + adam_eps) + weight_decay * master
        )
        new_moment_ref[:, cols] = new_moment
        new_second_ref[:, cols] = new_second


def front_kernel(
    group, y_rows, span_ref, place_ref, b_ref, own_ref, mate_ref, logit_ref, stat_ref, row_ref
):
    ctx, y_place, vocab_place = place_ref[0], place_ref[1], place_ref[2]
    tok = own_ref.shape[1]
    span = tok // 2
    quads = b_ref.shape[2] // NC
    small_ref = b_ref.at[:, :, :, b_ref.shape[3] - 2 * tok :]
    left, right = [], []
    for offset in (0, 1):
        sid = span_ref[2 * ctx + offset]
        at_z = (sid >> 2) & (NZ - 1)
        at_y = (y_place - (sid >> 5)) & (NY - 1)
        chip = small_ref[at_z, at_y].astype(f32)
        mine = jnp.where((sid & 2) == 0, chip[:quads], chip[quads:])
        odd = (sid & 1) == 1
        left.append(jnp.where(odd, mine[:, span:tok], mine[:, :span]))
        right.append(jnp.where(odd, mine[:, tok + span :], mine[:, tok : tok + span]))
    left = jnp.concatenate(left, 1)
    right = jnp.concatenate(right, 1)
    marks = jnp.sum(small_ref[:, :, :, :tok].astype(f32), axis=(0, 1))
    marks = marks[2:3] + marks[quads + 2 : quads + 3]
    token_count = jnp.sum(marks, axis=1, keepdims=True)
    target = left[0:1] * 256.0 + left[1:2]
    mask = left[2:3]
    local = target.astype(jnp.int32) - group * 4 - vocab_place * group
    ids = lax.broadcasted_iota(jnp.int32, (group, tok), 0)
    within = ids & (y_rows - 1)
    ids = ((y_place * y_rows - (ids - within)) & (group - 1)) + within
    hits = ids == local
    logits = own_ref[...] + mate_ref[...]
    logit_ref[...] = logits
    top = jnp.max(logits, axis=0, keepdims=True)
    stat_ref[0:1, :] = top
    stat_ref[1:2, :] = jnp.sum(jnp.exp(logits - top), axis=0, keepdims=True)
    stat_ref[2:3, :] = jnp.sum(jnp.where(hits, logits, 0.0), axis=0, keepdims=True)
    stat_ref[3:8, :] = jnp.zeros((5, tok), f32)
    row_ref[0:1, :] = target
    row_ref[1:2, :] = mask
    row_ref[2:3, :] = left[3:4] + right[0:1] + right[1:2]
    row_ref[3:4, :] = right[2:3] + right[3:4]
    row_ref[4:5, :] = mask * (loss_scale / token_count)
    row_ref[5:6, :] = jnp.broadcast_to(1.0 / token_count, (1, tok))
    row_ref[6:8, :] = jnp.zeros((2, tok), f32)


def square_kernel(a_ref, b0_ref, b1_ref, b2_ref, b3_ref, share_ref, grad_ref, report_ref):
    wide = a_ref.shape[2]
    part_a = a_ref[0].astype(f32)
    for i in range(1, a_ref.shape[0]):
        part_a = part_a + a_ref[i].astype(f32)
    part_b = b0_ref[...].astype(f32) + b1_ref[...].astype(f32)
    part_b = part_b + b2_ref[...].astype(f32) + b3_ref[...].astype(f32)
    grad_ref[:, :wide] = part_a
    grad_ref[:, wide:] = part_b
    total = jnp.sum(part_a * part_a, axis=1, keepdims=True)
    total = total + jnp.sum(part_b * part_b, axis=1, keepdims=True)
    total = jnp.sum(total, axis=0, keepdims=True)
    share = share_ref[...]
    row = jnp.concatenate([jnp.broadcast_to(total, share.shape), share], 1)
    report_ref[...] = jnp.broadcast_to(row[None], report_ref.shape)


VMEM = pl.BlockSpec(memory_space=pltpu.VMEM)
SMEM = pl.BlockSpec(memory_space=pltpu.SMEM)


def step(
    hidden_states, master, moment, second, targets, loss_mask, prior_lse, prior_target, span_order
):
    tok_rows, feat = hidden_states.shape
    shard_rows = master.shape[0]
    vocab_count = lax.axis_size("vocab")
    ctx_count = NY * NZ * NC
    core = lax.axis_index("core")
    y_place = lax.axis_index("y")
    vocab_place = lax.axis_index("vocab")
    ctx_place = (y_place * NZ + lax.axis_index("z")) * NC + core
    span = tok_rows // 2
    half = feat // 2
    group_rows = shard_rows * ctx_count
    block_total = group_rows * vocab_count
    y_rows = group_rows // NY
    chip_rows = y_rows // NZ

    thin = half // 16
    wide = half - thin
    thin_g = half * 3 // 16
    wide_g = half - thin_g
    halves = master.astype(bf16).reshape(shard_rows, NC, half)
    cut = halves[:, :, :wide].transpose(1, 0, 2)
    cut = jnp.broadcast_to(cut[None], (NZ,) + cut.shape).reshape(NZ * NC, shard_rows, wide)
    block = exchange(cut, ("z", "core")).reshape(y_rows, wide)
    digit = 256
    pieces = [targets // digit, targets % digit, loss_mask]
    pieces = [p.astype(f32) for p in pieces] + split(prior_lse, 3) + split(prior_target, 2)
    small = jnp.concatenate(
        [jnp.stack(pieces[:4], 0), jnp.stack(pieces[4:], 0)], 1
    ).astype(bf16)
    near_b = lax.dynamic_index_in_dim(halves[:, :, wide:], core, 1, keepdims=False)
    far_b = lax.dynamic_index_in_dim(halves[:, :, wide:], 1 - core, 1, keepdims=False)
    near_b = jnp.concatenate([near_b, small], 1)
    far_b = jnp.concatenate([far_b, small], 1)
    far_b = lax.ppermute(far_b, "core", SWAP)
    chip_b = pair(near_b, far_b, core == 0, 0)
    chips_b = jnp.stack([chip_b] + [shift(chip_b, "y", NY, s) for s in range(1, NY)], 0)
    parts_a = [block] + [shift(block, "y", NY, s) for s in range(1, NY)]
    part_b = spread(chips_b, "z", NZ)
    slot_ids = jnp.arange(span_order.shape[0], dtype=jnp.int32)
    slots = [
        jnp.sum(jnp.where(span_order == 2 * ctx_place + offset, slot_ids, 0))
        for offset in (0, 1)
    ]
    at = jnp.arange(8, dtype=jnp.int32)
    place = jnp.where(at == 0, ctx_place, jnp.where(at == 1, y_place, vocab_place))
    place = jnp.where(at == 3, slots[0], jnp.where(at == 4, slots[1], place))
    place = lax.optimization_barrier(jnp.where(at == 5, core, place))
    own_half = lax.dynamic_slice(
        hidden_states, (0, core * half), (tok_rows, half), allow_negative_indices=False
    )
    far_half = lax.dynamic_slice(
        hidden_states, (0, (1 - core) * half), (tok_rows, half), allow_negative_indices=False
    )
    mate_half = lax.ppermute(far_half, "core", SWAP)
    tokens = jnp.concatenate([own_half, mate_half], 0)

    head, own_part, mate_part = pl.pallas_call(
        functools.partial(score_kernel, thin),
        out_shape=(
            jax.ShapeDtypeStruct((group_rows, half), bf16),
            jax.ShapeDtypeStruct((group_rows, tok_rows), f32),
            jax.ShapeDtypeStruct((group_rows, tok_rows), f32),
        ),
        in_specs=[VMEM] * (NY + 3),
        out_specs=(VMEM, VMEM, VMEM),
        name="score",
    )(*parts_a, part_b, own_half, mate_half)
    mate_part = lax.ppermute(mate_part, "core", SWAP)
    mate_head = lax.ppermute(head, "core", SWAP)
    logits, stats, rows = pl.pallas_call(
        functools.partial(front_kernel, group_rows, y_rows),
        out_shape=(
            jax.ShapeDtypeStruct((group_rows, tok_rows), f32),
            jax.ShapeDtypeStruct((8, tok_rows), f32),
            jax.ShapeDtypeStruct((8, tok_rows), f32),
        ),
        in_specs=[SMEM, SMEM, VMEM, VMEM, VMEM],
        out_specs=(VMEM, VMEM, VMEM),
        name="front",
    )(span_order, place, part_b, own_part, mate_part)
    tgt_rows = rows[0].astype(jnp.int32)
    mask_rows, prior_rows, outside, mask_scale = rows[1], rows[2], rows[3], rows[4]
    local_col = tgt_rows - block_total - vocab_place * group_rows
    vocab_ids = lax.broadcasted_iota(jnp.int32, (group_rows, tok_rows), 0)
    within = vocab_ids & (y_rows - 1)
    vocab_ids = ((y_place * y_rows - (vocab_ids - within)) & (group_rows - 1)) + within
    hits = vocab_ids == local_col[None, :]
    heard = [stats] + [shift(stats, "vocab", vocab_count, s) for s in range(1, vocab_count)]
    ordered = []
    for j in range(vocab_count):
        back = (vocab_place - j) % vocab_count
        pick = heard[0]
        for s in range(1, vocab_count):
            pick = jnp.where(back == s, heard[s], pick)
        ordered.append(pick)
    stats = jnp.stack(ordered, 0)
    top_value = jnp.maximum(prior_rows, jnp.max(stats[:, 0], axis=0))
    sum_total = jnp.sum(stats[:, 1] * jnp.exp(stats[:, 0] - top_value[None, :]), axis=0)
    target_sum = jnp.sum(stats[:, 2], axis=0)
    log_total = top_value + jnp.log(jnp.exp(prior_rows - top_value) + sum_total)
    target_logit = jnp.where(tgt_rows >= block_total, target_sum, outside)
    loss_rows = mask_rows * (log_total - target_logit)
    dlogits = (
        mask_scale[None, :] * (jnp.exp(logits - log_total[None, :]) - hits.astype(f32))
    ).astype(bf16)
    mate_dlogits = lax.ppermute(dlogits, "core", SWAP)

    both = jnp.concatenate([dlogits, mate_dlogits], 1)
    partial_rows = jnp.dot(both, tokens, preferred_element_type=f32).astype(bf16)
    blocks = [partial_rows[s * y_rows : (s + 1) * y_rows, :wide_g] for s in range(NY)]
    by_y = blocks[0].astype(f32)
    for s in range(1, NY):
        by_y = by_y + shift(blocks[s], "y", NY, -s).astype(f32)
    by_y = by_y.astype(bf16).reshape(NZ, chip_rows, wide_g)
    by_z = partial_rows[:, wide_g:].reshape(NY, NZ, chip_rows, thin_g).transpose(1, 0, 2, 3)
    by_z = jnp.sum(exchange(by_z, "z").astype(f32), axis=0).astype(bf16)
    pieces_b = [by_z[0]] + [shift(by_z[s], "y", NY, -s) for s in range(1, NY)]
    pieces_a = exchange(by_y, "z")
    lanes = tok_rows // vocab_count
    share = lax.dynamic_slice_in_dim(loss_rows, vocab_place * lanes, lanes, 0)
    share = share[None]
    chip_grad, report = pl.pallas_call(
        square_kernel,
        out_shape=(
            jax.ShapeDtypeStruct((chip_rows, half), f32),
            jax.ShapeDtypeStruct((ctx_count * vocab_count, 1, 2 * lanes), f32),
        ),
        in_specs=[VMEM] * (NY + 2),
        out_specs=(VMEM, VMEM),
        name="square",
    )(pieces_a, *pieces_b, share)
    reports = exchange(report, ALL)
    near = lax.dynamic_slice_in_dim(chip_grad, core * shard_rows, shard_rows, 0)
    far = lax.dynamic_slice_in_dim(chip_grad, (1 - core) * shard_rows, shard_rows, 0)
    mate = lax.ppermute(far, "core", SWAP)

    width = feat // vocab_count
    per_half = vocab_count // NC
    hidden_parts = []
    for s in range(vocab_count - 1, -1, -1):
        q = (vocab_place + s) & (vocab_count - 1)
        at = (q & (per_half - 1)) * width
        side = jnp.where(
            (q >= per_half) == (core == 1),
            lax.dynamic_slice(head, (0, at), (group_rows, width), allow_negative_indices=False),
            lax.dynamic_slice(
                mate_head, (0, at), (group_rows, width), allow_negative_indices=False
            ),
        )
        if s == 2:
            side = lax.optimization_barrier(side)
        part = lax.dot_general(
            dlogits, side, (((0,), (0,)), ((), ())), preferred_element_type=f32
        ).astype(bf16)
        if s:
            part = shift(part, "vocab", vocab_count, s)
        else:
            part = lax.optimization_barrier(part)
        hidden_parts.append(part)
    hidden_grad = sum(part.astype(f32) for part in hidden_parts).astype(bf16)

    state = jax.ShapeDtypeStruct((shard_rows, feat), f32)
    token_loss, mean_loss, new_master, new_moment, new_second = pl.pallas_call(
        final_kernel,
        out_shape=(
            jax.ShapeDtypeStruct((2, span), f32),
            jax.ShapeDtypeStruct((1, 1), f32),
            state,
            state,
            state,
        ),
        in_specs=[SMEM] + [VMEM] * 7,
        out_specs=(VMEM,) * 5,
        name="final",
    )(place, reports, rows, near, mate, master, moment, second)
    token_loss = token_loss.reshape(tok_rows)
    mean_loss = mean_loss[0, 0]
    return (token_loss, mean_loss, hidden_grad, new_master, new_moment, new_second)


def solution(mesh):
    grid = Mesh(mesh.devices.reshape(NY, NZ, NC, mesh.devices.shape[1]), ALL)
    head_spec = P(("vocab",) + CTX, None)
    in_specs = (
        P(CTX, None),
        head_spec,
        head_spec,
        head_spec,
        P(CTX),
        P(CTX),
        P(CTX),
        P(CTX),
        P(),
    )
    out_specs = (P(CTX), P(), P(CTX, "vocab"), head_spec, head_spec, head_spec)
    return jax.shard_map(step, mesh=grid, in_specs=in_specs, out_specs=out_specs, check_vma=False)
```

```python
import functools

import jax
import jax.numpy as jnp
from jax import lax
from jax.experimental import pallas as pl
from jax.experimental.pallas import tpu as pltpu
from jax.sharding import Mesh, PartitionSpec as P


loss_scale = 1048576.0
clip_norm = 0.004
beta_one = 0.9
beta_two = 0.95
learn_rate = 0.001
weight_decay = 0.1
adam_eps = 1e-08

NY, NZ, NC = 4, 8, 2
CTX = ("y", "z", "core")
ALL = ("y", "z", "core", "vocab")
SWAP = [(0, 1), (1, 0)]
f32 = jnp.float32
bf16 = jnp.bfloat16


def exchange(x, axes):
    return lax.all_to_all(x, axes, 0, 0, tiled=True)


def shift(x, axis, count, step):
    return lax.ppermute(x, axis, [(i, (i + step) % count) for i in range(count)])


def pair(x, y, keep, axis):
    return jnp.where(keep, jnp.concatenate([x, y], axis), jnp.concatenate([y, x], axis))


def split(x, count):
    out = []
    for _ in range(count):
        out.append(lax.reduce_precision(x, 8, 7))
        x = x - out[-1]
    return out


def spread(x, axes, count):
    return exchange(jnp.broadcast_to(x[None], (count,) + x.shape), axes)


def score_kernel(
    thin, a0_ref, a1_ref, a2_ref, a3_ref, b_ref, tok_ref,
    head_out_ref, own_part_ref, mate_part_ref, head_ref, held_ref, sems,
):
    y_rows, wide = a0_ref.shape
    rows = tok_ref.shape[0] // 2
    blocks = [
        pltpu.make_async_copy(
            a_ref, head_ref.at[pl.ds(s * y_rows, y_rows), pl.ds(0, wide)], sems.at[s]
        )
        for s, a_ref in enumerate((a0_ref, a1_ref, a2_ref, a3_ref))
    ]
    mate_copy, own_copy = [
        pltpu.make_async_copy(
            tok_ref.at[pl.ds(at, rows)], held_ref.at[pl.ds(at, rows)], sems.at[sem]
        )
        for at, sem in ((rows, NY), (0, NY + 1))
    ]
    for copy in blocks:
        copy.start()
    mate_copy.start()
    own_copy.start()
    for s in range(NY):
        for z in range(NZ):
            at = s * y_rows + z * (y_rows // NZ)
            head_ref[at : at + y_rows // NZ, wide:] = b_ref[z, s, :, :thin]
    for copy in blocks:
        copy.wait()
    out_copy = pltpu.make_async_copy(head_ref, head_out_ref, sems.at[NY + 2])
    out_copy.start()
    mate_copy.wait()
    mate_part_ref[...] = lax.dot_general(
        head_ref[...], held_ref[rows:], (((1,), (1,)), ((), ())), preferred_element_type=f32
    )
    own_copy.wait()
    own_part_ref[...] = lax.dot_general(
        head_ref[...], held_ref[:rows], (((1,), (1,)), ((), ())), preferred_element_type=f32
    )
    out_copy.wait()


def final_kernel(
    place_ref, report_ref, row_ref, near_ref, mate_ref, master_ref, moment_ref, second_ref,
    loss_ref, mean_ref, new_master_ref, new_moment_ref, new_second_ref,
):
    sums = jnp.sum(report_ref[...], axis=0)
    norm_value = jnp.sqrt(sums[0:1, 0:1]) / loss_scale
    clip_factor = jnp.minimum(1.0, clip_norm / (norm_value + 1e-06))
    lanes = report_ref.shape[2] // 2
    mean_ref[...] = jnp.sum(sums[:, lanes:], axis=1, keepdims=True) * row_ref[5:6, 0:1]
    for i in (0, 1):
        slot = place_ref[3 + i]
        for j in (0, 1):
            loss_ref[i : i + 1, j * lanes : (j + 1) * lanes] = report_ref[2 * slot + j, :, lanes:]
    half = near_ref.shape[1]
    for h in (0, 1):
        cols = slice(h * half, (h + 1) * half)
        row_grad = jnp.where(place_ref[5] == h, near_ref[...], mate_ref[...])
        clipped = row_grad * clip_factor
        new_moment = beta_one * moment_ref[:, cols] + (1.0 - beta_one) * clipped
        new_second = beta_two * second_ref[:, cols] + (1.0 - beta_two) * clipped * clipped
        master = master_ref[:, cols]
        new_master_ref[:, cols] = master - learn_rate * (
            new_moment / (jnp.sqrt(new_second) + adam_eps) + weight_decay * master
        )
        new_moment_ref[:, cols] = new_moment
        new_second_ref[:, cols] = new_second


def front_kernel(
    group, y_rows, span_ref, place_ref, b_ref, own_ref, mate_ref, logit_ref, stat_ref, row_ref
):
    ctx, y_place, vocab_place = place_ref[0], place_ref[1], place_ref[2]
    tok = own_ref.shape[1]
    span = tok // 2
    quads = b_ref.shape[2] // NC
    small_ref = b_ref.at[:, :, :, b_ref.shape[3] - 2 * tok :]
    left, right = [], []
    for offset in (0, 1):
        sid = span_ref[2 * ctx + offset]
        at_z = (sid >> 2) & (NZ - 1)
        at_y = (y_place - (sid >> 5)) & (NY - 1)
        chip = small_ref[at_z, at_y].astype(f32)
        mine = jnp.where((sid & 2) == 0, chip[:quads], chip[quads:])
        odd = (sid & 1) == 1
        left.append(jnp.where(odd, mine[:, span:tok], mine[:, :span]))
        right.append(jnp.where(odd, mine[:, tok + span :], mine[:, tok : tok + span]))
    left = jnp.concatenate(left, 1)
    right = jnp.concatenate(right, 1)
    marks = jnp.sum(small_ref[:, :, :, :tok].astype(f32), axis=(0, 1))
    marks = marks[2:3] + marks[quads + 2 : quads + 3]
    token_count = jnp.sum(marks, axis=1, keepdims=True)
    target = left[0:1] * 256.0 + left[1:2]
    mask = left[2:3]
    local = target.astype(jnp.int32) - group * 4 - vocab_place * group
    ids = lax.broadcasted_iota(jnp.int32, (group, tok), 0)
    within = ids & (y_rows - 1)
    ids = ((y_place * y_rows - (ids - within)) & (group - 1)) + within
    hits = ids == local
    logits = own_ref[...] + mate_ref[...]
    logit_ref[...] = logits
    top = jnp.max(logits, axis=0, keepdims=True)
    stat_ref[0:1, :] = top
    stat_ref[1:2, :] = jnp.sum(jnp.exp(logits - top), axis=0, keepdims=True)
    stat_ref[2:3, :] = jnp.sum(jnp.where(hits, logits, 0.0), axis=0, keepdims=True)
    stat_ref[3:8, :] = jnp.zeros((5, tok), f32)
    row_ref[0:1, :] = target
    row_ref[1:2, :] = mask
    row_ref[2:3, :] = left[3:4] + right[0:1] + right[1:2]
    row_ref[3:4, :] = right[2:3] + right[3:4]
    row_ref[4:5, :] = mask * (loss_scale / token_count)
    row_ref[5:6, :] = jnp.broadcast_to(1.0 / token_count, (1, tok))
    row_ref[6:8, :] = jnp.zeros((2, tok), f32)


def square_kernel(a_ref, b0_ref, b1_ref, b2_ref, b3_ref, share_ref, grad_ref, report_ref):
    wide = a_ref.shape[2]
    part_a = a_ref[0].astype(f32)
    for i in range(1, a_ref.shape[0]):
        part_a = part_a + a_ref[i].astype(f32)
    part_b = b0_ref[...].astype(f32) + b1_ref[...].astype(f32)
    part_b = part_b + b2_ref[...].astype(f32) + b3_ref[...].astype(f32)
    grad_ref[:, :wide] = part_a
    grad_ref[:, wide:] = part_b
    total = jnp.sum(part_a * part_a, axis=1, keepdims=True)
    total = total + jnp.sum(part_b * part_b, axis=1, keepdims=True)
    total = jnp.sum(total, axis=0, keepdims=True)
    share = share_ref[...]
    row = jnp.concatenate([jnp.broadcast_to(total, share.shape), share], 1)
    report_ref[...] = jnp.broadcast_to(row[None], report_ref.shape)


VMEM = pl.BlockSpec(memory_space=pltpu.VMEM)
ANY = pl.BlockSpec(memory_space=pl.ANY)
SMEM = pl.BlockSpec(memory_space=pltpu.SMEM)


def step(
    hidden_states, master, moment, second, targets, loss_mask, prior_lse, prior_target, span_order
):
    tok_rows, feat = hidden_states.shape
    shard_rows = master.shape[0]
    vocab_count = lax.axis_size("vocab")
    ctx_count = NY * NZ * NC
    core = lax.axis_index("core")
    y_place = lax.axis_index("y")
    vocab_place = lax.axis_index("vocab")
    ctx_place = (y_place * NZ + lax.axis_index("z")) * NC + core
    span = tok_rows // 2
    half = feat // 2
    group_rows = shard_rows * ctx_count
    block_total = group_rows * vocab_count
    y_rows = group_rows // NY
    chip_rows = y_rows // NZ

    thin = half // 16
    wide = half - thin
    thin_g = half * 3 // 16
    wide_g = half - thin_g
    halves = master.astype(bf16).reshape(shard_rows, NC, half)
    cut = halves[:, :, :wide].transpose(1, 0, 2)
    cut = jnp.broadcast_to(cut[None], (NZ,) + cut.shape).reshape(NZ * NC, shard_rows, wide)
    block = exchange(cut, ("z", "core")).reshape(y_rows, wide)
    digit = 256
    pieces = [targets // digit, targets % digit, loss_mask]
    pieces = [p.astype(f32) for p in pieces] + split(prior_lse, 3) + split(prior_target, 2)
    small = jnp.concatenate(
        [jnp.stack(pieces[:4], 0), jnp.stack(pieces[4:], 0)], 1
    ).astype(bf16)
    near_b = lax.dynamic_index_in_dim(halves[:, :, wide:], core, 1, keepdims=False)
    far_b = lax.dynamic_index_in_dim(halves[:, :, wide:], 1 - core, 1, keepdims=False)
    near_b = jnp.concatenate([near_b, small], 1)
    far_b = jnp.concatenate([far_b, small], 1)
    far_b = lax.ppermute(far_b, "core", SWAP)
    chip_b = pair(near_b, far_b, core == 0, 0)
    chips_b = jnp.stack([chip_b] + [shift(chip_b, "y", NY, s) for s in range(1, NY)], 0)
    parts_a = [block] + [shift(block, "y", NY, s) for s in range(1, NY)]
    part_b = spread(chips_b, "z", NZ)
    slot_ids = jnp.arange(span_order.shape[0], dtype=jnp.int32)
    slots = [
        jnp.sum(jnp.where(span_order == 2 * ctx_place + offset, slot_ids, 0))
        for offset in (0, 1)
    ]
    at = jnp.arange(8, dtype=jnp.int32)
    place = jnp.where(at == 0, ctx_place, jnp.where(at == 1, y_place, vocab_place))
    place = jnp.where(at == 3, slots[0], jnp.where(at == 4, slots[1], place))
    place = lax.optimization_barrier(jnp.where(at == 5, core, place))
    own_half = lax.dynamic_slice(
        hidden_states, (0, core * half), (tok_rows, half), allow_negative_indices=False
    )
    far_half = lax.dynamic_slice(
        hidden_states, (0, (1 - core) * half), (tok_rows, half), allow_negative_indices=False
    )
    mate_half = lax.ppermute(far_half, "core", SWAP)
    tokens = lax.optimization_barrier(jnp.concatenate([own_half, mate_half], 0))

    head, own_part, mate_part = pl.pallas_call(
        functools.partial(score_kernel, thin),
        out_shape=(
            jax.ShapeDtypeStruct((group_rows, half), bf16),
            jax.ShapeDtypeStruct((group_rows, tok_rows), f32),
            jax.ShapeDtypeStruct((group_rows, tok_rows), f32),
        ),
        in_specs=[ANY] * NY + [VMEM, ANY],
        out_specs=(ANY, VMEM, VMEM),
        scratch_shapes=[
            pltpu.VMEM((group_rows, half), bf16),
            pltpu.VMEM((NC * tok_rows, half), bf16),
            pltpu.SemaphoreType.DMA((NY + 3,)),
        ],
        name="score",
    )(*parts_a, part_b, tokens)
    mate_part = lax.ppermute(mate_part, "core", SWAP)
    mate_head = lax.ppermute(head, "core", SWAP)
    logits, stats, rows = pl.pallas_call(
        functools.partial(front_kernel, group_rows, y_rows),
        out_shape=(
            jax.ShapeDtypeStruct((group_rows, tok_rows), f32),
            jax.ShapeDtypeStruct((8, tok_rows), f32),
            jax.ShapeDtypeStruct((8, tok_rows), f32),
        ),
        in_specs=[SMEM, SMEM, VMEM, VMEM, VMEM],
        out_specs=(VMEM, VMEM, VMEM),
        name="front",
    )(span_order, place, part_b, own_part, mate_part)
    tgt_rows = rows[0].astype(jnp.int32)
    mask_rows, prior_rows, outside, mask_scale = rows[1], rows[2], rows[3], rows[4]
    local_col = tgt_rows - block_total - vocab_place * group_rows
    vocab_ids = lax.broadcasted_iota(jnp.int32, (group_rows, tok_rows), 0)
    within = vocab_ids & (y_rows - 1)
    vocab_ids = ((y_place * y_rows - (vocab_ids - within)) & (group_rows - 1)) + within
    hits = vocab_ids == local_col[None, :]
    heard = [stats] + [shift(stats, "vocab", vocab_count, s) for s in range(1, vocab_count)]
    ordered = []
    for j in range(vocab_count):
        back = (vocab_place - j) % vocab_count
        pick = heard[0]
        for s in range(1, vocab_count):
            pick = jnp.where(back == s, heard[s], pick)
        ordered.append(pick)
    stats = jnp.stack(ordered, 0)
    top_value = jnp.maximum(prior_rows, jnp.max(stats[:, 0], axis=0))
    sum_total = jnp.sum(stats[:, 1] * jnp.exp(stats[:, 0] - top_value[None, :]), axis=0)
    target_sum = jnp.sum(stats[:, 2], axis=0)
    log_total = top_value + jnp.log(jnp.exp(prior_rows - top_value) + sum_total)
    target_logit = jnp.where(tgt_rows >= block_total, target_sum, outside)
    loss_rows = mask_rows * (log_total - target_logit)
    dlogits = (
        mask_scale[None, :] * (jnp.exp(logits - log_total[None, :]) - hits.astype(f32))
    ).astype(bf16)
    mate_dlogits = lax.ppermute(dlogits, "core", SWAP)

    both = jnp.concatenate([dlogits, mate_dlogits], 1)
    partial_rows = jnp.dot(both, tokens, preferred_element_type=f32).astype(bf16)
    blocks = [partial_rows[s * y_rows : (s + 1) * y_rows, :wide_g] for s in range(NY)]
    by_y = blocks[0].astype(f32)
    for s in range(1, NY):
        by_y = by_y + shift(blocks[s], "y", NY, -s).astype(f32)
    by_y = by_y.astype(bf16).reshape(NZ, chip_rows, wide_g)
    by_z = partial_rows[:, wide_g:].reshape(NY, NZ, chip_rows, thin_g).transpose(1, 0, 2, 3)
    by_z = jnp.sum(exchange(by_z, "z").astype(f32), axis=0).astype(bf16)
    pieces_b = [by_z[0]] + [shift(by_z[s], "y", NY, -s) for s in range(1, NY)]
    pieces_a = exchange(by_y, "z")
    lanes = tok_rows // vocab_count
    share = lax.dynamic_slice_in_dim(loss_rows, vocab_place * lanes, lanes, 0)
    share = share[None]
    chip_grad, report = pl.pallas_call(
        square_kernel,
        out_shape=(
            jax.ShapeDtypeStruct((chip_rows, half), f32),
            jax.ShapeDtypeStruct((ctx_count * vocab_count, 1, 2 * lanes), f32),
        ),
        in_specs=[VMEM] * (NY + 2),
        out_specs=(VMEM, VMEM),
        name="square",
    )(pieces_a, *pieces_b, share)
    reports = exchange(report, ALL)
    near = lax.dynamic_slice_in_dim(chip_grad, core * shard_rows, shard_rows, 0)
    far = lax.dynamic_slice_in_dim(chip_grad, (1 - core) * shard_rows, shard_rows, 0)
    mate = lax.ppermute(far, "core", SWAP)

    width = feat // vocab_count
    per_half = vocab_count // NC
    hidden_parts = []
    for s in range(vocab_count - 1, -1, -1):
        q = (vocab_place + s) & (vocab_count - 1)
        at = (q & (per_half - 1)) * width
        side = jnp.where(
            (q >= per_half) == (core == 1),
            lax.dynamic_slice(head, (0, at), (group_rows, width), allow_negative_indices=False),
            lax.dynamic_slice(
                mate_head, (0, at), (group_rows, width), allow_negative_indices=False
            ),
        )
        if s == 2:
            side = lax.optimization_barrier(side)
        part = lax.dot_general(
            dlogits, side, (((0,), (0,)), ((), ())), preferred_element_type=f32
        ).astype(bf16)
        if s:
            part = shift(part, "vocab", vocab_count, s)
        else:
            part = lax.optimization_barrier(part)
        hidden_parts.append(part)
    hidden_grad = sum(part.astype(f32) for part in hidden_parts).astype(bf16)

    state = jax.ShapeDtypeStruct((shard_rows, feat), f32)
    token_loss, mean_loss, new_master, new_moment, new_second = pl.pallas_call(
        final_kernel,
        out_shape=(
            jax.ShapeDtypeStruct((2, span), f32),
            jax.ShapeDtypeStruct((1, 1), f32),
            state,
            state,
            state,
        ),
        in_specs=[SMEM] + [VMEM] * 7,
        out_specs=(VMEM,) * 5,
        name="final",
    )(place, reports, rows, near, mate, master, moment, second)
    token_loss = token_loss.reshape(tok_rows)
    mean_loss = mean_loss[0, 0]
    return (token_loss, mean_loss, hidden_grad, new_master, new_moment, new_second)


def solution(mesh):
    grid = Mesh(mesh.devices.reshape(NY, NZ, NC, mesh.devices.shape[1]), ALL)
    head_spec = P(("vocab",) + CTX, None)
    in_specs = (
        P(CTX, None),
        head_spec,
        head_spec,
        head_spec,
        P(CTX),
        P(CTX),
        P(CTX),
        P(CTX),
        P(),
    )
    out_specs = (P(CTX), P(), P(CTX, "vocab"), head_spec, head_spec, head_spec)
    return jax.shard_map(step, mesh=grid, in_specs=in_specs, out_specs=out_specs, check_vma=False)
```

```python
import functools

import jax
import jax.numpy as jnp
from jax import lax
from jax.experimental import pallas as pl
from jax.experimental.pallas import tpu as pltpu
from jax.sharding import Mesh, PartitionSpec as P


loss_scale = 1048576.0
clip_norm = 0.004
beta_one = 0.9
beta_two = 0.95
learn_rate = 0.001
weight_decay = 0.1
adam_eps = 1e-08

NY, NZ, NC = 4, 8, 2
CTX = ("y", "z", "core")
ALL = ("y", "z", "core", "vocab")
SWAP = [(0, 1), (1, 0)]
f32 = jnp.float32
bf16 = jnp.bfloat16


def exchange(x, axes):
    return lax.all_to_all(x, axes, 0, 0, tiled=True)


def shift(x, axis, count, step):
    return lax.ppermute(x, axis, [(i, (i + step) % count) for i in range(count)])


def pair(x, y, keep, axis):
    return jnp.where(keep, jnp.concatenate([x, y], axis), jnp.concatenate([y, x], axis))


def split(x, count):
    out = []
    for _ in range(count):
        out.append(lax.reduce_precision(x, 8, 7))
        x = x - out[-1]
    return out


def spread(x, axes, count):
    return exchange(jnp.broadcast_to(x[None], (count,) + x.shape), axes)


def score_kernel(
    thin, a0_ref, a1_ref, a2_ref, a3_ref, b_ref, tok_ref, head_ref, own_part_ref, mate_part_ref
):
    wide = a0_ref.shape[1]
    y_rows = a0_ref.shape[0]
    for s, a_ref in enumerate((a0_ref, a1_ref, a2_ref, a3_ref)):
        head_ref[s * y_rows : (s + 1) * y_rows, :wide] = a_ref[...]
        for z in range(NZ):
            at = s * y_rows + z * (y_rows // NZ)
            head_ref[at : at + y_rows // NZ, wide:] = b_ref[z, s, :, :thin]
    rows = tok_ref.shape[0] // 2
    for at, part_ref in ((rows, mate_part_ref), (0, own_part_ref)):
        part_ref[...] = lax.dot_general(
            head_ref[...], tok_ref[at : at + rows], (((1,), (1,)), ((), ())), preferred_element_type=f32
        )


def final_kernel(
    place_ref, report_ref, row_ref, near_ref, mate_ref, master_ref, moment_ref, second_ref,
    loss_ref, mean_ref, new_master_ref, new_moment_ref, new_second_ref,
):
    sums = jnp.sum(report_ref[...], axis=0)
    norm_value = jnp.sqrt(sums[0:1, 0:1]) / loss_scale
    clip_factor = jnp.minimum(1.0, clip_norm / (norm_value + 1e-06))
    lanes = report_ref.shape[2] // 2
    mean_ref[...] = jnp.sum(sums[:, lanes:], axis=1, keepdims=True) * row_ref[5:6, 0:1]
    for i in (0, 1):
        slot = place_ref[3 + i]
        for j in (0, 1):
            loss_ref[i : i + 1, j * lanes : (j + 1) * lanes] = report_ref[2 * slot + j, :, lanes:]
    half = near_ref.shape[1]
    for h in (0, 1):
        cols = slice(h * half, (h + 1) * half)
        row_grad = jnp.where(place_ref[5] == h, near_ref[...], mate_ref[...])
        clipped = row_grad * clip_factor
        new_moment = beta_one * moment_ref[:, cols] + (1.0 - beta_one) * clipped
        new_second = beta_two * second_ref[:, cols] + (1.0 - beta_two) * clipped * clipped
        master = master_ref[:, cols]
        new_master_ref[:, cols] = master - learn_rate * (
            new_moment / (jnp.sqrt(new_second) + adam_eps) + weight_decay * master
        )
        new_moment_ref[:, cols] = new_moment
        new_second_ref[:, cols] = new_second


def front_kernel(
    group, y_rows, span_ref, place_ref, b_ref, own_ref, mate_ref, logit_ref, stat_ref, row_ref
):
    ctx, y_place, vocab_place = place_ref[0], place_ref[1], place_ref[2]
    tok = own_ref.shape[1]
    span = tok // 2
    quads = b_ref.shape[2] // NC
    small_ref = b_ref.at[:, :, :, b_ref.shape[3] - 2 * tok :]
    left, right = [], []
    for offset in (0, 1):
        sid = span_ref[2 * ctx + offset]
        at_z = (sid >> 2) & (NZ - 1)
        at_y = (y_place - (sid >> 5)) & (NY - 1)
        chip = small_ref[at_z, at_y].astype(f32)
        mine = jnp.where((sid & 2) == 0, chip[:quads], chip[quads:])
        odd = (sid & 1) == 1
        left.append(jnp.where(odd, mine[:, span:tok], mine[:, :span]))
        right.append(jnp.where(odd, mine[:, tok + span :], mine[:, tok : tok + span]))
    left = jnp.concatenate(left, 1)
    right = jnp.concatenate(right, 1)
    marks = jnp.sum(small_ref[:, :, :, :tok].astype(f32), axis=(0, 1))
    marks = marks[2:3] + marks[quads + 2 : quads + 3]
    token_count = jnp.sum(marks, axis=1, keepdims=True)
    target = left[0:1] * 256.0 + left[1:2]
    mask = left[2:3]
    local = target.astype(jnp.int32) - group * 4 - vocab_place * group
    ids = lax.broadcasted_iota(jnp.int32, (group, tok), 0)
    within = ids & (y_rows - 1)
    ids = ((y_place * y_rows - (ids - within)) & (group - 1)) + within
    hits = ids == local
    logits = own_ref[...] + mate_ref[...]
    logit_ref[...] = logits
    top = jnp.max(logits, axis=0, keepdims=True)
    stat_ref[0:1, :] = top
    stat_ref[1:2, :] = jnp.sum(jnp.exp(logits - top), axis=0, keepdims=True)
    stat_ref[2:3, :] = jnp.sum(jnp.where(hits, logits, 0.0), axis=0, keepdims=True)
    stat_ref[3:8, :] = jnp.zeros((5, tok), f32)
    row_ref[0:1, :] = target
    row_ref[1:2, :] = mask
    row_ref[2:3, :] = left[3:4] + right[0:1] + right[1:2]
    row_ref[3:4, :] = right[2:3] + right[3:4]
    row_ref[4:5, :] = mask * (loss_scale / token_count)
    row_ref[5:6, :] = jnp.broadcast_to(1.0 / token_count, (1, tok))
    row_ref[6:8, :] = jnp.zeros((2, tok), f32)


def square_kernel(a_ref, b0_ref, b1_ref, b2_ref, b3_ref, share_ref, grad_ref, report_ref):
    wide = a_ref.shape[2]
    part_a = a_ref[0].astype(f32)
    for i in range(1, a_ref.shape[0]):
        part_a = part_a + a_ref[i].astype(f32)
    part_b = b0_ref[...].astype(f32) + b1_ref[...].astype(f32)
    part_b = part_b + b2_ref[...].astype(f32) + b3_ref[...].astype(f32)
    grad_ref[:, :wide] = part_a
    grad_ref[:, wide:] = part_b
    total = jnp.sum(part_a * part_a, axis=1, keepdims=True)
    total = total + jnp.sum(part_b * part_b, axis=1, keepdims=True)
    total = jnp.sum(total, axis=0, keepdims=True)
    share = share_ref[...]
    row = jnp.concatenate([jnp.broadcast_to(total, share.shape), share], 1)
    report_ref[...] = jnp.broadcast_to(row[None], report_ref.shape)


VMEM = pl.BlockSpec(memory_space=pltpu.VMEM)
SMEM = pl.BlockSpec(memory_space=pltpu.SMEM)


def step(
    hidden_states, master, moment, second, targets, loss_mask, prior_lse, prior_target, span_order
):
    tok_rows, feat = hidden_states.shape
    shard_rows = master.shape[0]
    vocab_count = lax.axis_size("vocab")
    ctx_count = NY * NZ * NC
    core = lax.axis_index("core")
    y_place = lax.axis_index("y")
    vocab_place = lax.axis_index("vocab")
    ctx_place = (y_place * NZ + lax.axis_index("z")) * NC + core
    span = tok_rows // 2
    half = feat // 2
    group_rows = shard_rows * ctx_count
    block_total = group_rows * vocab_count
    y_rows = group_rows // NY
    chip_rows = y_rows // NZ

    thin = half // 16
    wide = half - thin
    thin_g = half * 3 // 16
    wide_g = half - thin_g
    halves = master.astype(bf16).reshape(shard_rows, NC, half)
    cut = master.astype(bf16)
    cut = jnp.stack([cut[:, i * half : i * half + wide] for i in range(NC)] * NZ, 0)
    block = exchange(cut, ("z", "core")).reshape(y_rows, wide)
    digit = 256
    pieces = [targets // digit, targets % digit, loss_mask]
    pieces = [p.astype(f32) for p in pieces] + split(prior_lse, 3) + split(prior_target, 2)
    small = jnp.concatenate(
        [jnp.stack(pieces[:4], 0), jnp.stack(pieces[4:], 0)], 1
    ).astype(bf16)
    near_b = lax.dynamic_index_in_dim(halves[:, :, wide:], core, 1, keepdims=False)
    far_b = lax.dynamic_index_in_dim(halves[:, :, wide:], 1 - core, 1, keepdims=False)
    near_b = jnp.concatenate([near_b, small], 1)
    far_b = jnp.concatenate([far_b, small], 1)
    far_b = lax.ppermute(far_b, "core", SWAP)
    chip_b = pair(near_b, far_b, core == 0, 0)
    chips_b = jnp.stack([chip_b] + [shift(chip_b, "y", NY, s) for s in range(1, NY)], 0)
    parts_a = [block] + [shift(block, "y", NY, s) for s in range(1, NY)]
    part_b = spread(chips_b, "z", NZ)
    slot_ids = jnp.arange(span_order.shape[0], dtype=jnp.int32)
    slots = [
        jnp.sum(jnp.where(span_order == 2 * ctx_place + offset, slot_ids, 0))
        for offset in (0, 1)
    ]
    at = jnp.arange(8, dtype=jnp.int32)
    place = jnp.where(at == 0, ctx_place, jnp.where(at == 1, y_place, vocab_place))
    place = jnp.where(at == 3, slots[0], jnp.where(at == 4, slots[1], place))
    place = lax.optimization_barrier(jnp.where(at == 5, core, place))
    own_half = lax.dynamic_slice(
        hidden_states, (0, core * half), (tok_rows, half), allow_negative_indices=False
    )
    far_half = lax.dynamic_slice(
        hidden_states, (0, (1 - core) * half), (tok_rows, half), allow_negative_indices=False
    )
    mate_half = lax.ppermute(far_half, "core", SWAP)
    tokens = lax.optimization_barrier(jnp.concatenate([own_half, mate_half], 0))

    head, own_part, mate_part = pl.pallas_call(
        functools.partial(score_kernel, thin),
        out_shape=(
            jax.ShapeDtypeStruct((group_rows, half), bf16),
            jax.ShapeDtypeStruct((group_rows, tok_rows), f32),
            jax.ShapeDtypeStruct((group_rows, tok_rows), f32),
        ),
        in_specs=[VMEM] * (NY + 2),
        out_specs=(VMEM, VMEM, VMEM),
        name="score",
    )(*parts_a, part_b, tokens)
    mate_part = lax.ppermute(mate_part, "core", SWAP)
    mate_head = lax.ppermute(head, "core", SWAP)
    logits, stats, rows = pl.pallas_call(
        functools.partial(front_kernel, group_rows, y_rows),
        out_shape=(
            jax.ShapeDtypeStruct((group_rows, tok_rows), f32),
            jax.ShapeDtypeStruct((8, tok_rows), f32),
            jax.ShapeDtypeStruct((8, tok_rows), f32),
        ),
        in_specs=[SMEM, SMEM, VMEM, VMEM, VMEM],
        out_specs=(VMEM, VMEM, VMEM),
        name="front",
    )(span_order, place, part_b, own_part, mate_part)
    tgt_rows = rows[0].astype(jnp.int32)
    mask_rows, prior_rows, outside, mask_scale = rows[1], rows[2], rows[3], rows[4]
    local_col = tgt_rows - block_total - vocab_place * group_rows
    vocab_ids = lax.broadcasted_iota(jnp.int32, (group_rows, tok_rows), 0)
    within = vocab_ids & (y_rows - 1)
    vocab_ids = ((y_place * y_rows - (vocab_ids - within)) & (group_rows - 1)) + within
    hits = vocab_ids == local_col[None, :]
    heard = [stats] + [shift(stats, "vocab", vocab_count, s) for s in range(1, vocab_count)]
    ordered = []
    for j in range(vocab_count):
        back = (vocab_place - j) % vocab_count
        pick = heard[0]
        for s in range(1, vocab_count):
            pick = jnp.where(back == s, heard[s], pick)
        ordered.append(pick)
    stats = jnp.stack(ordered, 0)
    top_value = jnp.maximum(prior_rows, jnp.max(stats[:, 0], axis=0))
    sum_total = jnp.sum(stats[:, 1] * jnp.exp(stats[:, 0] - top_value[None, :]), axis=0)
    target_sum = jnp.sum(stats[:, 2], axis=0)
    log_total = top_value + jnp.log(jnp.exp(prior_rows - top_value) + sum_total)
    target_logit = jnp.where(tgt_rows >= block_total, target_sum, outside)
    loss_rows = mask_rows * (log_total - target_logit)
    dlogits = (
        mask_scale[None, :] * (jnp.exp(logits - log_total[None, :]) - hits.astype(f32))
    ).astype(bf16)
    mate_dlogits = lax.ppermute(dlogits, "core", SWAP)

    both = jnp.concatenate([dlogits, mate_dlogits], 1)
    partial_rows = jnp.dot(both, tokens, preferred_element_type=f32).astype(bf16)
    blocks = [partial_rows[s * y_rows : (s + 1) * y_rows, :wide_g] for s in range(NY)]
    by_y = blocks[0].astype(f32)
    for s in range(1, NY):
        by_y = by_y + shift(blocks[s], "y", NY, -s).astype(f32)
    by_y = by_y.astype(bf16).reshape(NZ, chip_rows, wide_g)
    by_z = partial_rows[:, wide_g:].reshape(NY, NZ, chip_rows, thin_g).transpose(1, 0, 2, 3)
    by_z = jnp.sum(exchange(by_z, "z").astype(f32), axis=0).astype(bf16)
    pieces_b = [by_z[0]] + [shift(by_z[s], "y", NY, -s) for s in range(1, NY)]
    pieces_a = exchange(by_y, "z")
    lanes = tok_rows // vocab_count
    share = lax.dynamic_slice_in_dim(loss_rows, vocab_place * lanes, lanes, 0)
    share = share[None]
    chip_grad, report = pl.pallas_call(
        square_kernel,
        out_shape=(
            jax.ShapeDtypeStruct((chip_rows, half), f32),
            jax.ShapeDtypeStruct((ctx_count * vocab_count, 1, 2 * lanes), f32),
        ),
        in_specs=[VMEM] * (NY + 2),
        out_specs=(VMEM, VMEM),
        name="square",
    )(pieces_a, *pieces_b, share)
    reports = exchange(report, ALL)
    near = lax.dynamic_slice_in_dim(chip_grad, core * shard_rows, shard_rows, 0)
    far = lax.dynamic_slice_in_dim(chip_grad, (1 - core) * shard_rows, shard_rows, 0)
    mate = lax.ppermute(far, "core", SWAP)

    width = feat // vocab_count
    per_half = vocab_count // NC
    hidden_parts = []
    for s in range(vocab_count - 1, -1, -1):
        q = (vocab_place + s) & (vocab_count - 1)
        at = (q & (per_half - 1)) * width
        side = jnp.where(
            (q >= per_half) == (core == 1),
            lax.dynamic_slice(head, (0, at), (group_rows, width), allow_negative_indices=False),
            lax.dynamic_slice(
                mate_head, (0, at), (group_rows, width), allow_negative_indices=False
            ),
        )
        if s == 2:
            side = lax.optimization_barrier(side)
        part = lax.dot_general(
            dlogits, side, (((0,), (0,)), ((), ())), preferred_element_type=f32
        ).astype(bf16)
        if s:
            part = shift(part, "vocab", vocab_count, s)
        else:
            part = lax.optimization_barrier(part)
        hidden_parts.append(part)
    hidden_grad = sum(part.astype(f32) for part in hidden_parts).astype(bf16)

    state = jax.ShapeDtypeStruct((shard_rows, feat), f32)
    token_loss, mean_loss, new_master, new_moment, new_second = pl.pallas_call(
        final_kernel,
        out_shape=(
            jax.ShapeDtypeStruct((2, span), f32),
            jax.ShapeDtypeStruct((1, 1), f32),
            state,
            state,
            state,
        ),
        in_specs=[SMEM] + [VMEM] * 7,
        out_specs=(VMEM,) * 5,
        name="final",
    )(place, reports, rows, near, mate, master, moment, second)
    token_loss = token_loss.reshape(tok_rows)
    mean_loss = mean_loss[0, 0]
    return (token_loss, mean_loss, hidden_grad, new_master, new_moment, new_second)


def solution(mesh):
    grid = Mesh(mesh.devices.reshape(NY, NZ, NC, mesh.devices.shape[1]), ALL)
    head_spec = P(("vocab",) + CTX, None)
    in_specs = (
        P(CTX, None),
        head_spec,
        head_spec,
        head_spec,
        P(CTX),
        P(CTX),
        P(CTX),
        P(CTX),
        P(),
    )
    out_specs = (P(CTX), P(), P(CTX, "vocab"), head_spec, head_spec, head_spec)
    return jax.shard_map(step, mesh=grid, in_specs=in_specs, out_specs=out_specs, check_vma=False)
```
